128 devices in a mesh: atom: 16 (over y, x), mode: 8 (over z, core).
Axes of the slice: x: 4, y: 4, z: 4, core: 2. Of those that a mesh axis runs over, the one named last changes fastest.
Arguments:
- eigvec: bfloat16 [3, 4096, 2048], P(None, 'atom', 'mode'), may hold values from -0.0546875 to 0.0546875
- force: float32 [3, 3, 16, 4096], P(None, None, None, 'atom'), may hold values from -12 to 12
- bond: float32 [3, 16, 4096], P(None, None, 'atom'), may hold values from -6 to 6
- nbr: int32 [16, 4096], P(None, 'atom'), may hold values from 0 to 4095, as said below
- band: int32 [2, 2048], P(None, 'mode'), may hold values from 0 to 2048, as said below
- freq: float32 [2048], P('mode'), may hold values from 0.5 to 4, as said below
Outputs:
- diffusivity: float32 [2048], P('mode')
- conductivity: float32 [2048], P('mode')
The draws below stay inside these ranges and needn't reach their ends.
Inputs may be any that keep to these rules, and one draw needn't show every extreme that they name: `nbr`: each entry is an atom whose position in atom order differs from that of its own atom by 1 to 128, counted cyclically over the 4096 atoms; the distance 128 occurs in every draw. For every mode i: max(0, i - 128) <= band[0, i] <= i < band[1, i] <= min(2048, i + 129); both outer limits are reached at some mode. `freq`: strictly increasing along the modes.
All inputs are finite; a program needn't handle non-finite values.
Results may differ from the reference program's by a relative error of at most 0.00057.
Values may be sent and summed in bfloat16 or wider, within the bound.
A program may use at most 64 MiB of HBM per device.

```python
import math
import jax
import jax.numpy as jnp
from jax import lax

ATOM_DEV = 256
MODE_DEV = 256
NBR = 16
RIM = 128
HALF = 128
BROAD = 128
ATOMS = 4096
MODES = 2048
N_ATOM = 16
N_MODE = 8


def draw_nbr(key, part):
    first_key = jax.random.fold_in(key, 11)
    second_key = jax.random.fold_in(key, 12)
    third_key = jax.random.fold_in(key, 13)
    magnitude = jax.random.randint(first_key, (NBR, ATOMS), 1, RIM + 1)
    direction = 2 * jax.random.randint(second_key, (NBR, ATOMS), 0, 2) - 1
    chosen = jax.random.randint(third_key, (), 0, ATOMS)
    atom_ids = jnp.arange(ATOMS, dtype=jnp.int32)
    slot_ids = jnp.arange(NBR, dtype=jnp.int32)[:, None]
    magnitude = jnp.where((slot_ids == 0) & (atom_ids[None, :] == chosen), RIM, magnitude)
    return ((atom_ids[None, :] + direction * magnitude) % ATOMS).astype(jnp.int32)


def draw_band(key, part):
    lower_key = jax.random.fold_in(key, 21)
    upper_key = jax.random.fold_in(key, 22)
    chosen_key = jax.random.fold_in(key, 23)
    below = jax.random.randint(lower_key, (MODES,), 0, HALF + 1)
    above = jax.random.randint(upper_key, (MODES,), 0, HALF + 1)
    chosen = jax.random.randint(chosen_key, (), HALF, MODES - HALF - 1)
    mode_ids = jnp.arange(MODES, dtype=jnp.int32)
    below = jnp.where(mode_ids == chosen, HALF, below)
    above = jnp.where(mode_ids == chosen, HALF, above)
    lower_end = jnp.maximum(mode_ids - below, 0)
    upper_end = jnp.minimum(mode_ids + 1 + above, MODES)
    return jnp.stack([lower_end, upper_end]).astype(jnp.int32)


def draw_freq(key, part):
    spacing = jax.random.uniform(key, (MODES,), minval=0.2, maxval=1.8)
    rising = jnp.cumsum(spacing)
    return (0.5 + 3.5 * rising / rising[-1]).astype(jnp.float32)


def levels(stream_key, extent, shards, least, top_value):
    def one(dim, shards_of):
        steps = jax.random.uniform(jax.random.fold_in(jax.random.fold_in(stream_key, 6), dim), (shards_of,), jnp.float32, least / len(shards), top_value / len(shards))
        return jnp.repeat(jnp.exp(steps), extent[dim] // shards_of).reshape((-1,) + (1,) * (len(extent) - dim - 1))

    level = one(*shards[0])
    for cut in shards[1:]:
        level = level * one(*cut)
    return level


def centred(rng, extent, scale, most, shards=(), kind=jnp.bfloat16):
    array = scale * jax.random.normal(rng, extent, jnp.float32)
    if shards:
        array = array * levels(rng, extent, shards, -0.22, 0.18)
    return jnp.clip(array, -most, most).astype(kind)


def setup_inputs(seed: int = 0) -> dict:
    arg_keys = jax.random.split(jax.random.key(seed), 7)
    eigvec = centred(arg_keys[0], (3, ATOMS, MODES), ((3 * ATOMS) ** -0.5), 0.0546875, ((1, 16), (2, 8)))
    force = centred(arg_keys[1], (3, 3, NBR, ATOMS), 2.0, 12.0, ((3, 16),), jnp.float32)
    bond = centred(arg_keys[2], (3, NBR, ATOMS), 1.0, 6.0, ((2, 16),), jnp.float32)
    nbr = draw_nbr(jax.random.fold_in(arg_keys[6], 71), 0)
    band = draw_band(jax.random.fold_in(arg_keys[6], 71), 0)
    freq = draw_freq(jax.random.fold_in(arg_keys[6], 71), 0)
    return {"eigvec": eigvec, "force": force, "bond": bond, "nbr": nbr, "band": band, "freq": freq}


def capacity_of(spectral):
    return spectral * spectral * jnp.exp(spectral) / (jnp.expm1(spectral) ** 2)


def pair_weight(own_freq, partner_freq, own_ids, partner_ids, lower_end, upper_end, broaden):
    inside = (partner_ids[:, None] >= lower_end[None, :]) & (partner_ids[:, None] < upper_end[None, :]) & (partner_ids[:, None] != own_ids[None, :])
    detune = own_freq[None, :] - partner_freq[:, None]
    lorentz = (broaden / math.pi) / (detune * detune + broaden * broaden)
    factor = (own_freq[None, :] + partner_freq[:, None]) ** 2 / (4.0 * own_freq[None, :] * partner_freq[:, None])
    return jnp.where(inside, lorentz * factor, 0.0)


def reference(eigvec, force, bond, nbr, band, freq):
    mode_count = MODE_DEV * N_MODE
    partner_span = MODE_DEV + 2 * HALF
    broaden = BROAD * (jnp.max(freq) - jnp.min(freq)) / (mode_count - 1)
    padded_freq = jnp.pad(freq, (HALF, HALF), constant_values=1.0)

    def one_block(block_index):
        mode_start = block_index * MODE_DEV
        own_columns = lax.dynamic_slice_in_dim(eigvec, mode_start, MODE_DEV, 2)

        def atom_step(atom_block, running_pair):
            atom_start = (atom_block * ATOM_DEV).astype(jnp.int32)
            eig_rows = lax.dynamic_slice_in_dim(eigvec, atom_start, ATOM_DEV, 1)
            wide_rows = jnp.pad(eig_rows, ((0, 0), (0, 0), (HALF, HALF)))
            partner_rows = lax.dynamic_slice_in_dim(wide_rows, mode_start, partner_span, 2)
            neighbours = lax.dynamic_slice_in_dim(nbr, atom_start, ATOM_DEV, 1)
            gathered = jnp.take(own_columns, neighbours, axis=1)
            force_rows = lax.dynamic_slice_in_dim(force, atom_start, ATOM_DEV, 3)
            bond_rows = lax.dynamic_slice_in_dim(bond, atom_start, ATOM_DEV, 2)
            coupling = (bond_rows[:, None, None] * force_rows[None]).astype(jnp.bfloat16)
            flux_image = jnp.einsum("kcdna,dnai->kcai", coupling.astype(jnp.float32), gathered.astype(jnp.float32)).astype(jnp.bfloat16)
            return running_pair + jnp.einsum("caj,kcai->kji", partner_rows.astype(jnp.float32), flux_image.astype(jnp.float32))

        start_pair = jnp.zeros((3, partner_span, MODE_DEV), jnp.float32)
        pair_terms = lax.fori_loop(0, N_ATOM, atom_step, start_pair)
        strength = jnp.sum(pair_terms * pair_terms, axis=0)
        own_freq = lax.dynamic_slice_in_dim(freq, mode_start, MODE_DEV)
        partner_freq = lax.dynamic_slice_in_dim(padded_freq, mode_start, partner_span)
        own_ids = mode_start + jnp.arange(MODE_DEV, dtype=jnp.int32)
        partner_ids = mode_start - HALF + jnp.arange(partner_span, dtype=jnp.int32)
        lower_end = lax.dynamic_slice_in_dim(band[0], mode_start, MODE_DEV)
        upper_end = lax.dynamic_slice_in_dim(band[1], mode_start, MODE_DEV)
        weight = pair_weight(own_freq, partner_freq, own_ids, partner_ids, lower_end, upper_end, broaden)
        return math.pi / (3.0 * own_freq * own_freq) * jnp.sum(weight * strength, axis=0)

    diffusivity = lax.map(one_block, jnp.arange(N_MODE, dtype=jnp.int32)).reshape(mode_count)
    conductivity = jnp.cumsum(capacity_of(freq) * diffusivity) / MODE_DEV
    return diffusivity, conductivity
```

```python
import functools
import math

import jax
import jax.numpy as jnp
from jax import lax
from jax.experimental import pallas as pl
from jax.experimental.pallas import tpu as pltpu
from jax.sharding import PartitionSpec as P

ATOM_DEV = 256
MODE_DEV = 256
NBR = 16
RIM = 128
HALF = 128
BROAD = 128
GROUP = 16
GROUPS = ATOM_DEV // GROUP
REACH = ATOM_DEV + RIM
ROWS = 8
BF16 = jnp.bfloat16
F32 = jnp.float32
MESH = pl.DeviceIdType.MESH


def iota(shape, dim):
    return lax.broadcasted_iota(jnp.int32, shape, dim)


def contract(lhs, rhs, lhs_dim, rhs_dim):
    return lax.dot_general(
        lhs, rhs, (((lhs_dim,), (rhs_dim,)), ((), ())), preferred_element_type=F32
    )


def kernel(
    n_atom,
    n_mode,
    eig_hbm,
    force_hbm,
    bond_hbm,
    nbr_hbm,
    band_hbm,
    freq_hbm,
    diff_ref,
    cond_ref,
    eig,
    force,
    bond,
    nbr,
    band,
    spectrum,
    low_rows,
    high_rows,
    low_cols,
    high_cols,
    nbr_rows,
    hot,
    spread,
    own_m,
    rim_m,
    flux,
    eig_t,
    send_pair,
    recv_pair,
    freq_col,
    send_sum,
    recv_sum,
    send_total,
    recv_total,
    local_sem,
    row_send,
    row_recv,
    col_send,
    col_recv,
    freq_send,
    freq_recv,
    pair_send,
    pair_recv,
    sum_send,
    sum_recv,
    total_send,
    total_recv,
):
    me = lax.axis_index("atom")
    block = lax.axis_index("mode")
    atoms = n_atom * ATOM_DEV

    barrier = pltpu.get_barrier_semaphore()

    def greet_atom(q, carry):
        pl.semaphore_signal(
            barrier, inc=1, device_id=(lax.rem(me + q, n_atom), block), device_id_type=MESH
        )
        return carry

    def greet_mode(q, carry):
        pl.semaphore_signal(
            barrier, inc=1, device_id=(me, lax.rem(block + q, n_mode)), device_id_type=MESH
        )
        return carry

    lax.fori_loop(1, n_atom, greet_atom, 0)
    lax.fori_loop(1, n_mode, greet_mode, 0)

    loads = [
        pltpu.make_async_copy(nbr_hbm, nbr, local_sem.at[0]),
        pltpu.make_async_copy(bond_hbm, bond, local_sem.at[1]),
        pltpu.make_async_copy(force_hbm, force, local_sem.at[2]),
        pltpu.make_async_copy(eig_hbm, eig, local_sem.at[3]),
        pltpu.make_async_copy(band_hbm, band, local_sem.at[4]),
        pltpu.make_async_copy(freq_hbm, spectrum.at[pl.ds(0, 1), :], local_sem.at[5]),
    ]
    for load in loads:
        load.start()

    lane = iota((ATOM_DEV, 256), 1)
    diagonal = (iota((ATOM_DEV, 256), 0) & (GROUP - 1)) == (lane & (GROUP - 1))
    slot_rows = jnp.where(
        (iota((NBR, 256), 1) >> 4) == iota((NBR, 256), 0), 1.0, 0.0
    ).astype(BF16)

    loads[0].wait()
    place = ((nbr[...] - me * ATOM_DEV + RIM + atoms) & (atoms - 1)) - RIM
    column = jnp.where(place < 0, place + REACH, place)
    coarse = contract((column >> 4).astype(F32).astype(BF16), slot_rows, 0, 0)
    fine = contract((column & 15).astype(F32).astype(BF16), slot_rows, 0, 0)
    column_of = jnp.where(diagonal, coarse * 16.0 + fine, 0.0)
    nbr_rows[...] = jnp.sum(column_of.reshape(GROUPS, GROUP, 256), axis=1)

    loads[5].wait()
    loads[3].wait()
    pl.semaphore_wait(barrier, n_atom + n_mode - 2)

    def to_atom(src, dst, q, send, recv):
        return pltpu.make_async_remote_copy(
            src_ref=src,
            dst_ref=dst,
            send_sem=send,
            recv_sem=recv,
            device_id=(lax.rem(me + q, n_atom), block),
            device_id_type=MESH,
        )

    def to_mode(src, dst, q, send, recv):
        return pltpu.make_async_remote_copy(
            src_ref=src,
            dst_ref=dst,
            send_sem=send,
            recv_sem=recv,
            device_id=(me, lax.rem(block + q, n_mode)),
            device_id_type=MESH,
        )

    up_rows = to_atom(
        eig.at[:, pl.ds(ATOM_DEV - RIM, RIM), :], low_rows, 1, row_send.at[0], row_recv.at[0]
    )
    down_rows = to_atom(
        eig.at[:, pl.ds(0, RIM), :], high_rows, n_atom - 1, row_send.at[1], row_recv.at[1]
    )
    up_cols = to_mode(
        eig.at[:, :, pl.ds(MODE_DEV - HALF, HALF)], low_cols, 1, col_send.at[0], col_recv.at[0]
    )
    down_cols = to_mode(
        eig.at[:, :, pl.ds(0, HALF)], high_cols, n_mode - 1, col_send.at[1], col_recv.at[1]
    )
    up_rows.start()
    down_rows.start()

    @pl.when(block < n_mode - 1)
    def _():
        up_cols.start()

    @pl.when(block > 0)
    def _():
        down_cols.start()

    def send_freq(q, carry):
        to_mode(
            spectrum.at[pl.ds(0, 1), :],
            spectrum.at[pl.ds(q, 1), :],
            q,
            freq_send,
            freq_recv,
        ).start()
        return carry

    lax.fori_loop(1, n_mode, send_freq, 0)

    reach_rows = iota((REACH, 256), 0).astype(F32)

    def one_hot(g, carry):
        hot[g] = jnp.where(reach_rows == nbr_rows[pl.ds(g, 1), :], 1.0, 0.0).astype(BF16)
        return carry

    lax.fori_loop(0, GROUPS, one_hot, 0)

    loads[1].wait()
    loads[2].wait()

    def build(k):
        for c in range(3):
            for d in range(3):
                coupling = (bond[k] * force[c, d]).astype(BF16)
                wide = jnp.where(diagonal, contract(coupling, slot_rows, 0, 0), 0.0).astype(BF16)
                first = (3 * c + d) * GROUP
                spread[:, first : first + GROUP, :] = wide.reshape(GROUPS, GROUP, 256)

        def group(g, carry):
            dense = contract(spread[g], hot[g], 1, 1).astype(BF16)
            for c in range(3):
                for d in range(3):
                    first = (3 * c + d) * GROUP
                    part = dense[first : first + GROUP]
                    rows = pl.ds(pl.multiple_of(g * GROUP, GROUP), GROUP)
                    own_m[c, rows, d * ATOM_DEV : (d + 1) * ATOM_DEV] = part[:, :ATOM_DEV]
                    rim_m[c, rows, d * RIM : (d + 1) * RIM] = part[:, ATOM_DEV:]
            return carry

        lax.fori_loop(0, GROUPS, group, 0)

    row = iota((HALF, HALF), 0)
    col = iota((HALF, HALF), 1)

    def project(k):
        inner = contract(
            own_m[...].reshape(3 * ATOM_DEV, 3 * ATOM_DEV),
            eig[...].reshape(3 * ATOM_DEV, MODE_DEV),
            1,
            0,
        ).reshape(3, ATOM_DEV, MODE_DEV)
        for h, halo in enumerate((low_rows, high_rows)):
            outer = contract(
                rim_m[:, h * RIM : (h + 1) * RIM, :].reshape(3 * RIM, 3 * RIM),
                halo[...].reshape(3 * RIM, MODE_DEV),
                1,
                0,
            ).reshape(3, RIM, MODE_DEV)
            flux[:, h * RIM : (h + 1) * RIM, :] = (
                inner[:, h * RIM : (h + 1) * RIM, :] + outer
            ).astype(BF16)
        pair = contract(eig_t[...], flux[...].reshape(3 * ATOM_DEV, MODE_DEV), 1, 0)
        for h in range(2):
            ours = slice(h * HALF, (h + 1) * HALF)
            before = pair[h * HALF : (h + 1) * HALF, ours]
            level = pair[(h + 1) * HALF : (h + 2) * HALF, ours]
            after = pair[(h + 2) * HALF : (h + 3) * HALF, ours]
            outer = jnp.where(row > col, before, after)
            inner_part = jnp.where(row == col, before, level)
            send_pair[k, :, 2 * h] = outer.reshape(n_atom, ROWS, HALF)
            send_pair[k, :, 2 * h + 1] = inner_part.reshape(n_atom, ROWS, HALF)

        def send(q, carry):
            to_atom(
                send_pair.at[k, lax.rem(me + q, n_atom)],
                recv_pair.at[k, q - 1],
                q,
                pair_send.at[k],
                pair_recv.at[k],
            ).start()
            return carry

        lax.fori_loop(1, n_atom, send, 0)

    build(0)
    for c in range(3):
        eig_t[HALF : HALF + MODE_DEV, c * ATOM_DEV : (c + 1) * ATOM_DEV] = eig[c].T

    @pl.when(block > 0)
    def _():
        up_cols.wait_recv()

    @pl.when(block == 0)
    def _():
        low_cols[...] = jnp.zeros_like(low_cols)

    @pl.when(block < n_mode - 1)
    def _():
        down_cols.wait_recv()

    @pl.when(block == n_mode - 1)
    def _():
        high_cols[...] = jnp.zeros_like(high_cols)

    for c in range(3):
        eig_t[:HALF, c * ATOM_DEV : (c + 1) * ATOM_DEV] = low_cols[c].T
        eig_t[HALF + MODE_DEV :, c * ATOM_DEV : (c + 1) * ATOM_DEV] = high_cols[c].T
    up_rows.wait_recv()
    down_rows.wait_recv()
    project(0)
    build(1)
    project(1)
    build(2)
    project(2)

    loads[4].wait()
    pltpu.make_async_copy(
        spectrum.at[pl.ds(1, n_mode - 1), :], spectrum.at[pl.ds(1, n_mode - 1), :], freq_recv
    ).wait()
    own_freq = spectrum[pl.ds(0, 1), :]
    columns = spectrum[...].T
    freq_col[:HALF] = jnp.broadcast_to(columns[HALF:, 1:2], (HALF, HALF))
    freq_col[HALF : HALF + MODE_DEV] = jnp.broadcast_to(columns[:, 0:1], (MODE_DEV, HALF))
    freq_col[HALF + MODE_DEV :] = jnp.broadcast_to(
        columns[:HALF, n_mode - 1 : n_mode], (HALF, HALF)
    )
    every = spectrum[...]
    highest = jnp.max(jnp.max(every, axis=1, keepdims=True), axis=0, keepdims=True)
    lowest = jnp.min(jnp.min(every, axis=1, keepdims=True), axis=0, keepdims=True)
    broaden = BROAD * (highest - lowest) / (n_mode * MODE_DEV - 1)

    start = block * MODE_DEV
    first = me * ROWS
    rows = first + iota((ROWS, HALF), 0)
    lanes = iota((ROWS, HALF), 1)
    weights = []
    for h in range(2):
        ours = slice(h * HALF, (h + 1) * HALF)
        mine = own_freq[:, ours]
        lower = band[0:1, ours]
        upper = band[1:2, ours]

        def freq_at(offset):
            return freq_col[pl.ds(pl.multiple_of(offset + first, ROWS), ROWS), :]

        before = freq_at(h * HALF)
        level = freq_at((h + 1) * HALF)
        after = freq_at((h + 2) * HALF)
        base = start + h * HALF + rows
        for partner, ids in (
            (
                jnp.where(rows > lanes, before, after),
                base + jnp.where(rows > lanes, -HALF, HALF),
            ),
            (
                jnp.where(rows == lanes, before, level),
                base + jnp.where(rows == lanes, -HALF, 0),
            ),
        ):
            own_ids = start + h * HALF + lanes
            inside = (ids >= lower) & (ids < upper) & (ids != own_ids)
            detune = mine - partner
            lorentz = broaden / math.pi / (detune * detune + broaden * broaden)
            factor = (mine + partner) ** 2 / (4.0 * mine * partner)
            weights.append((inside, lorentz * factor))

    strength = jnp.zeros((4, ROWS, HALF), F32)
    for k in range(3):
        pltpu.make_async_copy(recv_pair.at[k], recv_pair.at[k], pair_recv.at[k]).wait()
        total = send_pair[k, me]
        for q in range(n_atom - 1):
            total = total + recv_pair[k, q]
        strength = strength + total * total

    for h in range(2):
        term = 0.0
        for s in range(2):
            inside, weight = weights[2 * h + s]
            term = term + jnp.where(inside, weight * strength[2 * h + s], 0.0)
        send_sum[h : h + 1] = jnp.sum(term, axis=0, keepdims=True)

    def share(q, carry):
        to_atom(send_sum, recv_sum.at[q - 1], q, sum_send, sum_recv).start()
        return carry

    lax.fori_loop(1, n_atom, share, 0)
    freq_two = jnp.concatenate([own_freq[:, :HALF], own_freq[:, HALF:]], axis=0)
    grown = jnp.exp(freq_two)
    capacity = freq_two * freq_two * grown / ((grown - 1.0) * (grown - 1.0))
    prefactor = math.pi / (3.0 * freq_two * freq_two)
    pltpu.make_async_copy(recv_sum, recv_sum, sum_recv).wait()
    row_sums = send_sum[...]
    for q in range(n_atom - 1):
        row_sums = row_sums + recv_sum[q]
    diffusivity = prefactor * row_sums
    diff_ref[...] = diffusivity
    running = capacity * diffusivity
    send_total[...] = jnp.broadcast_to(
        jnp.sum(jnp.sum(running, axis=1, keepdims=True), axis=0, keepdims=True), (1, HALF)
    )

    def share_total(q, carry):
        to_mode(send_total, recv_total.at[q - 1], q, total_send, total_recv).start()
        return carry

    lax.fori_loop(1, n_mode, share_total, 0)
    lane_two = iota((2, HALF), 1)
    for step in (1, 2, 4, 8, 16, 32, 64):
        running = running + jnp.where(lane_two >= step, pltpu.roll(running, step, 1), 0.0)
    low_total = running[0:1, HALF - 1 : HALF]
    running = running + jnp.where(iota((2, HALF), 0) == 1, low_total, 0.0)
    pltpu.make_async_copy(recv_total, recv_total, total_recv).wait()
    earlier = jnp.zeros((1, HALF), F32)
    for q in range(1, n_mode):
        earlier = earlier + jnp.where(block >= q, recv_total[q - 1], 0.0)
    cond_ref[...] = (earlier + running) / MODE_DEV

    up_rows.wait_send()
    down_rows.wait_send()

    @pl.when(block < n_mode - 1)
    def _():
        up_cols.wait_send()

    @pl.when(block > 0)
    def _():
        down_cols.wait_send()

    pltpu.make_async_copy(
        spectrum.at[pl.ds(1, n_mode - 1), :], spectrum.at[pl.ds(1, n_mode - 1), :], freq_send
    ).wait()
    for k in range(3):
        pltpu.make_async_copy(recv_pair.at[k], recv_pair.at[k], pair_send.at[k]).wait()
    pltpu.make_async_copy(recv_sum, recv_sum, sum_send).wait()
    pltpu.make_async_copy(recv_total, recv_total, total_send).wait()


def body(eigvec, force, bond, nbr, band, freq):
    n_atom, n_mode = lax.axis_size("atom"), lax.axis_size("mode")
    any_spec = pl.BlockSpec(memory_space=pl.ANY)
    vmem_spec = pl.BlockSpec(memory_space=pltpu.VMEM)
    dma = pltpu.SemaphoreType.DMA
    diffusivity, conductivity = pl.pallas_call(
        functools.partial(kernel, n_atom, n_mode),
        out_shape=(
            jax.ShapeDtypeStruct((2, HALF), F32),
            jax.ShapeDtypeStruct((2, HALF), F32),
        ),
        in_specs=[any_spec] * 6,
        out_specs=(vmem_spec, vmem_spec),
        scratch_shapes=[
            pltpu.VMEM((3, ATOM_DEV, MODE_DEV), BF16),
            pltpu.VMEM((3, 3, NBR, ATOM_DEV), F32),
            pltpu.VMEM((3, NBR, ATOM_DEV), F32),
            pltpu.VMEM((NBR, ATOM_DEV), jnp.int32),
            pltpu.VMEM((2, MODE_DEV), jnp.int32),
            pltpu.VMEM((n_mode, MODE_DEV), F32),
            pltpu.VMEM((3, RIM, MODE_DEV), BF16),
            pltpu.VMEM((3, RIM, MODE_DEV), BF16),
            pltpu.VMEM((3, ATOM_DEV, HALF), BF16),
            pltpu.VMEM((3, ATOM_DEV, HALF), BF16),
            pltpu.VMEM((GROUPS, 256), F32),
            pltpu.VMEM((GROUPS, REACH, 256), BF16),
            pltpu.VMEM((GROUPS, 9 * GROUP, 256), BF16),
            pltpu.VMEM((3, ATOM_DEV, 3 * ATOM_DEV), BF16),
            pltpu.VMEM((3, ATOM_DEV, 3 * RIM), BF16),
            pltpu.VMEM((3, ATOM_DEV, MODE_DEV), BF16),
            pltpu.VMEM((MODE_DEV + 2 * HALF, 3 * ATOM_DEV), BF16),
            pltpu.VMEM((3, n_atom, 4, ROWS, HALF), F32),
            pltpu.VMEM((3, n_atom - 1, 4, ROWS, HALF), F32),
            pltpu.VMEM((MODE_DEV + 2 * HALF, HALF), F32),
            pltpu.VMEM((2, HALF), F32),
            pltpu.VMEM((n_atom - 1, 2, HALF), F32),
            pltpu.VMEM((1, HALF), F32),
            pltpu.VMEM((n_mode - 1, 1, HALF), F32),
            dma((6,)),
            dma((2,)),
            dma((2,)),
            dma((2,)),
            dma((2,)),
            dma(()),
            dma(()),
            dma((3,)),
            dma((3,)),
            dma(()),
            dma(()),
            dma(()),
            dma(()),
        ],
        compiler_params=pltpu.CompilerParams(
            collective_id=0, has_side_effects=True, vmem_limit_bytes=63 * 1024 * 1024
        ),
    )(eigvec, force, bond, nbr, band, freq.reshape(1, MODE_DEV))
    return diffusivity.reshape(MODE_DEV), conductivity.reshape(MODE_DEV)


def solution(mesh):
    in_specs = (
        P(None, "atom", "mode"),
        P(None, None, None, "atom"),
        P(None, None, "atom"),
        P(None, "atom"),
        P(None, "mode"),
        P("mode"),
    )
    out_specs = (P("mode"), P("mode"))
    return jax.shard_map(body, mesh=mesh, in_specs=in_specs, out_specs=out_specs, check_vma=False)
```

```python
import functools
import math

import jax
import jax.numpy as jnp
from jax import lax
from jax.experimental import pallas as pl
from jax.experimental.pallas import tpu as pltpu
from jax.sharding import PartitionSpec as P

ATOM_DEV = 256
MODE_DEV = 256
NBR = 16
RIM = 128
HALF = 128
BROAD = 128
GROUP = 16
GROUPS = ATOM_DEV // GROUP
ROWS = 8
BF16 = jnp.bfloat16
F32 = jnp.float32
MESH = pl.DeviceIdType.MESH


def iota(shape, dim):
    return lax.broadcasted_iota(jnp.int32, shape, dim)


def contract(lhs, rhs, lhs_dim, rhs_dim):
    return lax.dot_general(
        lhs, rhs, (((lhs_dim,), (rhs_dim,)), ((), ())), preferred_element_type=F32
    )


def drain(ref, sem):
    pltpu.make_async_copy(ref, ref, sem).wait()


def kernel(
    n_atom,
    n_mode,
    eig_hbm,
    force_hbm,
    bond_hbm,
    nbr_hbm,
    band_hbm,
    freq_hbm,
    diff_ref,
    cond_ref,
    eig,
    force,
    bond,
    nbr,
    band,
    spectrum,
    low_rows,
    high_rows,
    low_cols,
    high_cols,
    nbr_cols,
    hot,
    spread,
    own_m,
    rim_m,
    flux,
    eig_t,
    send_pair,
    recv_pair,
    freq_col,
    send_sum,
    recv_sum,
    send_total,
    recv_total,
    local_sem,
    row_send,
    row_recv,
    col_send,
    col_recv,
    freq_send,
    freq_recv,
    pair_send,
    pair_recv,
    sum_send,
    sum_recv,
    total_send,
    total_recv,
):
    me = lax.axis_index("atom")
    block = lax.axis_index("mode")
    atoms = n_atom * ATOM_DEV

    barrier = pltpu.get_barrier_semaphore()

    def greet_atom(q, carry):
        pl.semaphore_signal(
            barrier, inc=1, device_id=(lax.rem(me + q, n_atom), block), device_id_type=MESH
        )
        return carry

    def greet_mode(q, carry):
        pl.semaphore_signal(
            barrier, inc=1, device_id=(me, lax.rem(block + q, n_mode)), device_id_type=MESH
        )
        return carry

    lax.fori_loop(1, n_atom, greet_atom, 0)
    lax.fori_loop(1, n_mode, greet_mode, 0)

    loads = [
        pltpu.make_async_copy(nbr_hbm, nbr, local_sem.at[0]),
        pltpu.make_async_copy(bond_hbm, bond, local_sem.at[1]),
        pltpu.make_async_copy(force_hbm, force, local_sem.at[2]),
        pltpu.make_async_copy(eig_hbm, eig, local_sem.at[3]),
        pltpu.make_async_copy(band_hbm, band, local_sem.at[4]),
        pltpu.make_async_copy(freq_hbm, spectrum.at[pl.ds(0, 1), :], local_sem.at[5]),
    ]
    for load in loads:
        load.start()

    lane = iota((ATOM_DEV, 256), 1)
    diagonal = (iota((ATOM_DEV, 256), 0) & (GROUP - 1)) == (lane & (GROUP - 1))
    slot_rows = jnp.where(
        (iota((NBR, 256), 1) >> 4) == iota((NBR, 256), 0), 1.0, 0.0
    ).astype(BF16)

    loads[0].wait()
    atom_ids = iota((NBR, ATOM_DEV), 1)
    offset = ((nbr[...] - me * ATOM_DEV - atom_ids + RIM + atoms) & (atoms - 1)) - RIM
    column = jnp.where(offset == RIM, atom_ids, (atom_ids + offset) & (ATOM_DEV - 1))
    nbr_cols[...] = column.astype(F32).T

    loads[5].wait()
    loads[3].wait()
    pl.semaphore_wait(barrier, n_atom + n_mode - 2)

    def to_atom(src, dst, q, send, recv):
        return pltpu.make_async_remote_copy(
            src_ref=src,
            dst_ref=dst,
            send_sem=send,
            recv_sem=recv,
            device_id=(lax.rem(me + q, n_atom), block),
            device_id_type=MESH,
        )

    def to_mode(src, dst, q, send, recv):
        return pltpu.make_async_remote_copy(
            src_ref=src,
            dst_ref=dst,
            send_sem=send,
            recv_sem=recv,
            device_id=(me, lax.rem(block + q, n_mode)),
            device_id_type=MESH,
        )

    up_rows = to_atom(
        eig.at[:, pl.ds(ATOM_DEV - RIM, RIM), :], low_rows, 1, row_send.at[0], row_recv.at[0]
    )
    down_rows = to_atom(
        eig.at[:, pl.ds(0, RIM), :], high_rows, n_atom - 1, row_send.at[1], row_recv.at[1]
    )
    up_cols = to_mode(
        eig.at[:, :, pl.ds(MODE_DEV - HALF, HALF)], low_cols, 1, col_send.at[0], col_recv.at[0]
    )
    down_cols = to_mode(
        eig.at[:, :, pl.ds(0, HALF)], high_cols, n_mode - 1, col_send.at[1], col_recv.at[1]
    )
    up_rows.start()
    down_rows.start()

    @pl.when(block < n_mode - 1)
    def _():
        up_cols.start()

    @pl.when(block > 0)
    def _():
        down_cols.start()

    def send_freq(q, carry):
        to_mode(
            spectrum.at[pl.ds(0, 1), :],
            spectrum.at[pl.ds(q, 1), :],
            q,
            freq_send,
            freq_recv,
        ).start()
        return carry

    lax.fori_loop(1, n_mode, send_freq, 0)

    col_ids = iota((GROUP, ATOM_DEV), 1).astype(F32)

    def one_hot(g, carry):
        own_cols = nbr_cols[pl.ds(pl.multiple_of(g * GROUP, GROUP), GROUP), :]
        for n in range(NBR):
            hot[g, n * GROUP : (n + 1) * GROUP, :] = jnp.where(
                own_cols[:, n : n + 1] == col_ids, 1.0, 0.0
            ).astype(BF16)
        return carry

    lax.fori_loop(0, GROUPS, one_hot, 0)

    loads[1].wait()
    loads[2].wait()

    def spread_out():
        for k in range(3):
            for c in range(3):
                for d in range(3):
                    coupling = (bond[k] * force[c, d]).astype(BF16)
                    wide = jnp.where(diagonal, contract(coupling, slot_rows, 0, 0), 0.0)
                    first = (9 * k + 3 * c + d) * GROUP
                    spread[:, first : first + GROUP, :] = wide.astype(BF16).reshape(
                        GROUPS, GROUP, 256
                    )

    near = iota((GROUP, RIM), 1) - iota((GROUP, RIM), 0)

    def unfold(h, g):
        dense = contract(spread[g], hot[g], 1, 0)
        gap = near - (g - h * (GROUPS // 2)) * GROUP
        below, same = gap < 0, gap == 0
        rows = pl.ds(pl.multiple_of(g * GROUP, GROUP), GROUP)
        for q in range(9):
            for d in range(3):
                first = (3 * q + d) * GROUP
                left = dense[first : first + GROUP, :RIM]
                right = dense[first : first + GROUP, RIM:]
                if h == 0:
                    own_left = jnp.where(same, 0.0, left)
                    own_right = jnp.where(below, right, jnp.where(same, left, 0.0))
                    rim = jnp.where(below, 0.0, right)
                else:
                    own_left = jnp.where(below, 0.0, left)
                    own_right = jnp.where(same, 0.0, right)
                    rim = jnp.where(below, left, jnp.where(same, right, 0.0))
                own_m[q, rows, d * ATOM_DEV : d * ATOM_DEV + RIM] = own_left.astype(BF16)
                own_m[q, rows, d * ATOM_DEV + RIM : (d + 1) * ATOM_DEV] = own_right.astype(BF16)
                rim_m[q, rows, d * RIM : (d + 1) * RIM] = rim.astype(BF16)

    def build():
        for h in range(2):

            def group(g, carry, h=h):
                unfold(h, g)
                return carry

            lax.fori_loop(h * (GROUPS // 2), (h + 1) * (GROUPS // 2), group, 0)

    row = iota((HALF, HALF), 0)
    col = iota((HALF, HALF), 1)

    def project(k):
        inner = contract(
            own_m[3 * k : 3 * k + 3].reshape(3 * ATOM_DEV, 3 * ATOM_DEV),
            eig[...].reshape(3 * ATOM_DEV, MODE_DEV),
            1,
            0,
        ).reshape(3, ATOM_DEV, MODE_DEV)
        for h, halo in enumerate((low_rows, high_rows)):
            outer = contract(
                rim_m[3 * k : 3 * k + 3, h * RIM : (h + 1) * RIM, :].reshape(3 * RIM, 3 * RIM),
                halo[...].reshape(3 * RIM, MODE_DEV),
                1,
                0,
            ).reshape(3, RIM, MODE_DEV)
            flux[:, h * RIM : (h + 1) * RIM, :] = (
                inner[:, h * RIM : (h + 1) * RIM, :] + outer
            ).astype(BF16)
        pair = contract(eig_t[...], flux[...].reshape(3 * ATOM_DEV, MODE_DEV), 1, 0)
        for h in range(2):
            ours = slice(h * HALF, (h + 1) * HALF)
            before = pair[h * HALF : (h + 1) * HALF, ours]
            level = pair[(h + 1) * HALF : (h + 2) * HALF, ours]
            after = pair[(h + 2) * HALF : (h + 3) * HALF, ours]
            outer = jnp.where(row > col, before, after)
            inner_part = jnp.where(row == col, before, level)
            send_pair[k, :, 2 * h] = outer.reshape(n_atom, ROWS, HALF)
            send_pair[k, :, 2 * h + 1] = inner_part.reshape(n_atom, ROWS, HALF)

        def send(q, carry):
            to_atom(
                send_pair.at[k, lax.rem(me + q, n_atom)],
                recv_pair.at[k, q - 1],
                q,
                pair_send.at[k],
                pair_recv.at[k],
            ).start()
            return carry

        lax.fori_loop(1, n_atom, send, 0)

    spread_out()
    build()
    for c in range(3):
        eig_t[HALF : HALF + MODE_DEV, c * ATOM_DEV : (c + 1) * ATOM_DEV] = eig[c].T

    @pl.when(block > 0)
    def _():
        up_cols.wait_recv()

    @pl.when(block == 0)
    def _():
        low_cols[...] = jnp.zeros_like(low_cols)

    @pl.when(block < n_mode - 1)
    def _():
        down_cols.wait_recv()

    @pl.when(block == n_mode - 1)
    def _():
        high_cols[...] = jnp.zeros_like(high_cols)

    for c in range(3):
        eig_t[:HALF, c * ATOM_DEV : (c + 1) * ATOM_DEV] = low_cols[c].T
        eig_t[HALF + MODE_DEV :, c * ATOM_DEV : (c + 1) * ATOM_DEV] = high_cols[c].T
    up_rows.wait_recv()
    down_rows.wait_recv()
    project(0)
    project(1)
    project(2)

    loads[4].wait()
    drain(spectrum.at[pl.ds(1, n_mode - 1), :], freq_recv)
    own_freq = spectrum[pl.ds(0, 1), :]
    columns = spectrum[...].T
    freq_col[:HALF] = jnp.broadcast_to(columns[HALF:, 1:2], (HALF, HALF))
    freq_col[HALF : HALF + MODE_DEV] = jnp.broadcast_to(columns[:, 0:1], (MODE_DEV, HALF))
    freq_col[HALF + MODE_DEV :] = jnp.broadcast_to(
        columns[:HALF, n_mode - 1 : n_mode], (HALF, HALF)
    )
    every = spectrum[...]
    highest = jnp.max(jnp.max(every, axis=1, keepdims=True), axis=0, keepdims=True)
    lowest = jnp.min(jnp.min(every, axis=1, keepdims=True), axis=0, keepdims=True)
    broaden = BROAD * (highest - lowest) / (n_mode * MODE_DEV - 1)

    start = block * MODE_DEV
    first = me * ROWS
    rows = first + iota((ROWS, HALF), 0)
    lanes = iota((ROWS, HALF), 1)
    weights = []
    for h in range(2):
        ours = slice(h * HALF, (h + 1) * HALF)
        mine = own_freq[:, ours]
        lower = band[0:1, ours]
        upper = band[1:2, ours]

        def freq_at(offset):
            return freq_col[pl.ds(pl.multiple_of(offset + first, ROWS), ROWS), :]

        before = freq_at(h * HALF)
        level = freq_at((h + 1) * HALF)
        after = freq_at((h + 2) * HALF)
        base = start + h * HALF + rows
        for partner, ids in (
            (
                jnp.where(rows > lanes, before, after),
                base + jnp.where(rows > lanes, -HALF, HALF),
            ),
            (
                jnp.where(rows == lanes, before, level),
                base + jnp.where(rows == lanes, -HALF, 0),
            ),
        ):
            own_ids = start + h * HALF + lanes
            inside = (ids >= lower) & (ids < upper) & (ids != own_ids)
            detune = mine - partner
            lorentz = broaden / math.pi / (detune * detune + broaden * broaden)
            factor = (mine + partner) ** 2 / (4.0 * mine * partner)
            weights.append((inside, lorentz * factor))

    strength = jnp.zeros((4, ROWS, HALF), F32)
    for k in range(3):
        drain(recv_pair.at[k], pair_recv.at[k])
        total = send_pair[k, me]
        for q in range(n_atom - 1):
            total = total + recv_pair[k, q]
        strength = strength + total * total

    for h in range(2):
        term = 0.0
        for s in range(2):
            inside, weight = weights[2 * h + s]
            term = term + jnp.where(inside, weight * strength[2 * h + s], 0.0)
        send_sum[h : h + 1] = jnp.sum(term, axis=0, keepdims=True)

    def share(q, carry):
        to_atom(send_sum, recv_sum.at[q - 1], q, sum_send, sum_recv).start()
        return carry

    lax.fori_loop(1, n_atom, share, 0)
    freq_two = jnp.concatenate([own_freq[:, :HALF], own_freq[:, HALF:]], axis=0)
    grown = jnp.exp(freq_two)
    capacity = freq_two * freq_two * grown / ((grown - 1.0) * (grown - 1.0))
    prefactor = math.pi / (3.0 * freq_two * freq_two)
    drain(recv_sum, sum_recv)
    row_sums = send_sum[...]
    for q in range(n_atom - 1):
        row_sums = row_sums + recv_sum[q]
    diffusivity = prefactor * row_sums
    diff_ref[...] = diffusivity
    running = capacity * diffusivity
    send_total[...] = jnp.broadcast_to(
        jnp.sum(jnp.sum(running, axis=1, keepdims=True), axis=0, keepdims=True), (1, HALF)
    )

    def share_total(q, carry):
        to_mode(send_total, recv_total.at[q - 1], q, total_send, total_recv).start()
        return carry

    lax.fori_loop(1, n_mode, share_total, 0)
    lane_two = iota((2, HALF), 1)
    for step in (1, 2, 4, 8, 16, 32, 64):
        running = running + jnp.where(lane_two >= step, pltpu.roll(running, step, 1), 0.0)
    low_total = running[0:1, HALF - 1 : HALF]
    running = running + jnp.where(iota((2, HALF), 0) == 1, low_total, 0.0)
    drain(recv_total, total_recv)
    earlier = jnp.zeros((1, HALF), F32)
    for q in range(1, n_mode):
        earlier = earlier + jnp.where(block >= q, recv_total[q - 1], 0.0)
    cond_ref[...] = (earlier + running) / MODE_DEV

    up_rows.wait_send()
    down_rows.wait_send()

    @pl.when(block < n_mode - 1)
    def _():
        up_cols.wait_send()

    @pl.when(block > 0)
    def _():
        down_cols.wait_send()

    drain(spectrum.at[pl.ds(1, n_mode - 1), :], freq_send)
    for k in range(3):
        drain(recv_pair.at[k], pair_send.at[k])
    drain(recv_sum, sum_send)
    drain(recv_total, total_send)


def body(eigvec, force, bond, nbr, band, freq):
    n_atom, n_mode = lax.axis_size("atom"), lax.axis_size("mode")
    any_spec = pl.BlockSpec(memory_space=pl.ANY)
    vmem_spec = pl.BlockSpec(memory_space=pltpu.VMEM)
    dma = pltpu.SemaphoreType.DMA
    diffusivity, conductivity = pl.pallas_call(
        functools.partial(kernel, n_atom, n_mode),
        out_shape=(
            jax.ShapeDtypeStruct((2, HALF), F32),
            jax.ShapeDtypeStruct((2, HALF), F32),
        ),
        in_specs=[any_spec] * 6,
        out_specs=(vmem_spec, vmem_spec),
        scratch_shapes=[
            pltpu.VMEM((3, ATOM_DEV, MODE_DEV), BF16),
            pltpu.VMEM((3, 3, NBR, ATOM_DEV), F32),
            pltpu.VMEM((3, NBR, ATOM_DEV), F32),
            pltpu.VMEM((NBR, ATOM_DEV), jnp.int32),
            pltpu.VMEM((2, MODE_DEV), jnp.int32),
            pltpu.VMEM((n_mode, MODE_DEV), F32),
            pltpu.VMEM((3, RIM, MODE_DEV), BF16),
            pltpu.VMEM((3, RIM, MODE_DEV), BF16),
            pltpu.VMEM((3, ATOM_DEV, HALF), BF16),
            pltpu.VMEM((3, ATOM_DEV, HALF), BF16),
            pltpu.VMEM((ATOM_DEV, NBR), F32),
            pltpu.VMEM((GROUPS, 256, ATOM_DEV), BF16),
            pltpu.VMEM((GROUPS, 27 * GROUP, 256), BF16),
            pltpu.VMEM((9, ATOM_DEV, 3 * ATOM_DEV), BF16),
            pltpu.VMEM((9, ATOM_DEV, 3 * RIM), BF16),
            pltpu.VMEM((3, ATOM_DEV, MODE_DEV), BF16),
            pltpu.VMEM((MODE_DEV + 2 * HALF, 3 * ATOM_DEV), BF16),
            pltpu.VMEM((3, n_atom, 4, ROWS, HALF), F32),
            pltpu.VMEM((3, n_atom - 1, 4, ROWS, HALF), F32),
            pltpu.VMEM((MODE_DEV + 2 * HALF, HALF), F32),
            pltpu.VMEM((2, HALF), F32),
            pltpu.VMEM((n_atom - 1, 2, HALF), F32),
            pltpu.VMEM((1, HALF), F32),
            pltpu.VMEM((n_mode - 1, 1, HALF), F32),
            dma((6,)),
            dma((2,)),
            dma((2,)),
            dma((2,)),
            dma((2,)),
            dma(()),
            dma(()),
            dma((3,)),
            dma((3,)),
            dma(()),
            dma(()),
            dma(()),
            dma(()),
        ],
        compiler_params=pltpu.CompilerParams(
            collective_id=0, has_side_effects=True, vmem_limit_bytes=63 * 1024 * 1024
        ),
    )(eigvec, force, bond, nbr, band, freq.reshape(1, MODE_DEV))
    return diffusivity.reshape(MODE_DEV), conductivity.reshape(MODE_DEV)


def solution(mesh):
    in_specs = (
        P(None, "atom", "mode"),
        P(None, None, None, "atom"),
        P(None, None, "atom"),
        P(None, "atom"),
        P(None, "mode"),
        P("mode"),
    )
    out_specs = (P("mode"), P("mode"))
    return jax.shard_map(body, mesh=mesh, in_specs=in_specs, out_specs=out_specs, check_vma=False)
```

```python
import functools
import math

import jax
import jax.numpy as jnp
from jax import lax
from jax.experimental import pallas as pl
from jax.experimental.pallas import tpu as pltpu
from jax.sharding import PartitionSpec as P

ATOM_DEV = 256
MODE_DEV = 256
NBR = 16
RIM = 128
HALF = 128
BROAD = 128
GROUP = 16
GROUPS = ATOM_DEV // GROUP
ROWS = 8
BF16 = jnp.bfloat16
F32 = jnp.float32
MESH = pl.DeviceIdType.MESH


def iota(shape, dim):
    return lax.broadcasted_iota(jnp.int32, shape, dim)


def contract(lhs, rhs, lhs_dim, rhs_dim):
    return lax.dot_general(
        lhs, rhs, (((lhs_dim,), (rhs_dim,)), ((), ())), preferred_element_type=F32
    )


def drain(ref, sem):
    pltpu.make_async_copy(ref, ref, sem).wait()


def kernel(
    n_atom,
    n_mode,
    eig_hbm,
    force_hbm,
    bond_hbm,
    nbr_hbm,
    band_hbm,
    freq_hbm,
    diff_ref,
    cond_ref,
    eig,
    force,
    bond,
    nbr,
    band,
    spectrum,
    low_rows,
    high_rows,
    low_cols,
    high_cols,
    nbr_cols,
    hot,
    spread,
    own_m,
    rim_m,
    flux,
    eig_t,
    send_pair,
    recv_pair,
    freq_col,
    send_sum,
    recv_sum,
    send_total,
    recv_total,
    inner_flux,
    local_sem,
    row_send,
    row_recv,
    col_send,
    col_recv,
    freq_send,
    freq_recv,
    pair_send,
    pair_recv,
    sum_send,
    sum_recv,
    total_send,
    total_recv,
    ready,
):
    me = lax.axis_index("atom")
    block = lax.axis_index("mode")
    atoms = n_atom * ATOM_DEV

    barrier = pltpu.get_barrier_semaphore()

    def greet_atom(q, carry):
        pl.semaphore_signal(
            barrier, inc=1, device_id=(lax.rem(me + q, n_atom), block), device_id_type=MESH
        )
        return carry

    recv_total[...] = jnp.zeros_like(recv_total)
    lax.fori_loop(1, n_atom, greet_atom, 0)

    def beside(shift, action):
        @pl.when(block + shift < n_mode)
        def _():
            action(block + shift)

        @pl.when(block - shift >= 0)
        def _():
            action(block - shift)

    def greet_mode(other):
        pl.semaphore_signal(barrier, inc=1, device_id=(me, other), device_id_type=MESH)

    beside(1, greet_mode)

    loads = [
        pltpu.make_async_copy(nbr_hbm, nbr, local_sem.at[0]),
        pltpu.make_async_copy(bond_hbm, bond, local_sem.at[1]),
        pltpu.make_async_copy(force_hbm, force, local_sem.at[2]),
        pltpu.make_async_copy(eig_hbm, eig, local_sem.at[3]),
        pltpu.make_async_copy(band_hbm, band, local_sem.at[4]),
        pltpu.make_async_copy(freq_hbm, spectrum.at[pl.ds(0, 1), :], local_sem.at[5]),
    ]
    for load in loads:
        load.start()

    lane = iota((ATOM_DEV, 256), 1)
    diagonal = (iota((ATOM_DEV, 256), 0) & (GROUP - 1)) == (lane & (GROUP - 1))
    slot_rows = jnp.where(
        (iota((NBR, 256), 1) >> 4) == iota((NBR, 256), 0), 1.0, 0.0
    ).astype(BF16)

    loads[0].wait()
    atom_ids = iota((NBR, ATOM_DEV), 1)
    offset = ((nbr[...] - me * ATOM_DEV - atom_ids + RIM + atoms) & (atoms - 1)) - RIM
    column = jnp.where(offset == RIM, atom_ids, (atom_ids + offset) & (ATOM_DEV - 1))
    nbr_cols[...] = column.astype(F32).T

    col_ids = iota((GROUP, ATOM_DEV), 1).astype(F32)

    def one_hot(g, carry):
        own_cols = nbr_cols[pl.ds(pl.multiple_of(g * GROUP, GROUP), GROUP), :]
        for n in range(NBR):
            hot[g, n * GROUP : (n + 1) * GROUP, :] = jnp.where(
                own_cols[:, n : n + 1] == col_ids, 1.0, 0.0
            ).astype(BF16)
        return carry

    lax.fori_loop(0, GROUPS, one_hot, 0)

    loads[5].wait()
    loads[3].wait()
    pl.semaphore_wait(
        barrier,
        n_atom - 1 + (block > 0).astype(jnp.int32) + (block < n_mode - 1).astype(jnp.int32),
    )

    def to_atom(src, dst, q, send, recv):
        return pltpu.make_async_remote_copy(
            src_ref=src,
            dst_ref=dst,
            send_sem=send,
            recv_sem=recv,
            device_id=(lax.rem(me + q, n_atom), block),
            device_id_type=MESH,
        )

    def to_mode(src, dst, q, send, recv):
        return pltpu.make_async_remote_copy(
            src_ref=src,
            dst_ref=dst,
            send_sem=send,
            recv_sem=recv,
            device_id=(me, lax.rem(block + q, n_mode)),
            device_id_type=MESH,
        )

    up_rows = to_atom(
        eig.at[:, pl.ds(ATOM_DEV - RIM, RIM), :], low_rows, 1, row_send.at[0], row_recv.at[0]
    )
    down_rows = to_atom(
        eig.at[:, pl.ds(0, RIM), :], high_rows, n_atom - 1, row_send.at[1], row_recv.at[1]
    )
    up_cols = to_mode(
        eig.at[:, :, pl.ds(MODE_DEV - HALF, HALF)], low_cols, 1, col_send.at[0], col_recv.at[0]
    )
    down_cols = to_mode(
        eig.at[:, :, pl.ds(0, HALF)], high_cols, n_mode - 1, col_send.at[1], col_recv.at[1]
    )
    up_rows.start()
    down_rows.start()

    @pl.when(block < n_mode - 1)
    def _():
        up_cols.start()

    @pl.when(block > 0)
    def _():
        down_cols.start()

    @pl.when(block > 0)
    def _():
        pl.semaphore_wait(ready.at[0], 1)

    @pl.when(block < n_mode - 1)
    def _():
        pl.semaphore_signal(
            ready.at[0], inc=1, device_id=(me, block + 1), device_id_type=MESH
        )

    def tell(other, carry):
        pl.semaphore_signal(ready.at[1], inc=1, device_id=(me, other), device_id_type=MESH)
        return carry

    lax.fori_loop(0, block, tell, 0)

    def send_freq(q, carry):
        to_mode(
            spectrum.at[pl.ds(0, 1), :],
            spectrum.at[pl.ds(q, 1), :],
            q,
            freq_send,
            freq_recv,
        ).start()
        return carry

    lax.fori_loop(n_mode - block, n_mode, send_freq, 0)

    loads[1].wait()
    loads[2].wait()

    def spread_out():
        for k in range(3):
            for c in range(3):
                for d in range(3):
                    coupling = (bond[k] * force[c, d]).astype(BF16)
                    wide = jnp.where(diagonal, contract(coupling, slot_rows, 0, 0), 0.0)
                    first = (9 * k + 3 * c + d) * GROUP
                    spread[:, first : first + GROUP, :] = wide.astype(BF16).reshape(
                        GROUPS, GROUP, 256
                    )

    near = iota((GROUP, RIM), 1) - iota((GROUP, RIM), 0)

    def unfold(h, g):
        dense = contract(spread[g], hot[g], 1, 0)
        gap = near - (g - h * (GROUPS // 2)) * GROUP
        below, same = gap < 0, gap == 0
        rows = pl.ds(pl.multiple_of(g * GROUP, GROUP), GROUP)
        for q in range(9):
            for d in range(3):
                first = (3 * q + d) * GROUP
                left = dense[first : first + GROUP, :RIM]
                right = dense[first : first + GROUP, RIM:]
                if h == 0:
                    own_left = jnp.where(same, 0.0, left)
                    own_right = jnp.where(below, right, jnp.where(same, left, 0.0))
                    rim = jnp.where(below, 0.0, right)
                else:
                    own_left = jnp.where(below, 0.0, left)
                    own_right = jnp.where(same, 0.0, right)
                    rim = jnp.where(below, left, jnp.where(same, right, 0.0))
                own_m[q, rows, d * ATOM_DEV : d * ATOM_DEV + RIM] = own_left.astype(BF16)
                own_m[q, rows, d * ATOM_DEV + RIM : (d + 1) * ATOM_DEV] = own_right.astype(BF16)
                rim_m[q, rows, d * RIM : (d + 1) * RIM] = rim.astype(BF16)

    def build():
        for h in range(2):

            def group(g, carry, h=h):
                unfold(h, g)
                return carry

            lax.fori_loop(h * (GROUPS // 2), (h + 1) * (GROUPS // 2), group, 0)

    row = iota((HALF, HALF), 0)
    col = iota((HALF, HALF), 1)

    def inner_part_of(k):
        inner_flux[3 * k : 3 * k + 3] = contract(
            own_m[3 * k : 3 * k + 3].reshape(3 * ATOM_DEV, 3 * ATOM_DEV),
            eig[...].reshape(3 * ATOM_DEV, MODE_DEV),
            1,
            0,
        ).reshape(3, ATOM_DEV, MODE_DEV)

    def project(k):
        for h, halo in enumerate((low_rows, high_rows)):
            outer = contract(
                rim_m[3 * k : 3 * k + 3, h * RIM : (h + 1) * RIM, :].reshape(3 * RIM, 3 * RIM),
                halo[...].reshape(3 * RIM, MODE_DEV),
                1,
                0,
            ).reshape(3, RIM, MODE_DEV)
            flux[:, h * RIM : (h + 1) * RIM, :] = (
                inner_flux[3 * k : 3 * k + 3, h * RIM : (h + 1) * RIM, :] + outer
            ).astype(BF16)
        pair = contract(eig_t[...], flux[...].reshape(3 * ATOM_DEV, MODE_DEV), 1, 0)
        for h in range(2):
            ours = slice(h * HALF, (h + 1) * HALF)
            before = pair[h * HALF : (h + 1) * HALF, ours]
            level = pair[(h + 1) * HALF : (h + 2) * HALF, ours]
            after = pair[(h + 2) * HALF : (h + 3) * HALF, ours]
            outer = jnp.where(row > col, before, after)
            inner_part = jnp.where(row == col, before, level)
            send_pair[k, :, 2 * h] = outer.reshape(n_atom, ROWS, HALF)
            send_pair[k, :, 2 * h + 1] = inner_part.reshape(n_atom, ROWS, HALF)

        def send(q, carry):
            to_atom(
                send_pair.at[k, lax.rem(me + q, n_atom)],
                recv_pair.at[k, q - 1],
                q,
                pair_send.at[k],
                pair_recv.at[k],
            ).start()
            return carry

        lax.fori_loop(1, n_atom, send, 0)

    spread_out()
    build()
    for k in range(3):
        inner_part_of(k)
    for c in range(3):
        eig_t[HALF : HALF + MODE_DEV, c * ATOM_DEV : (c + 1) * ATOM_DEV] = eig[c].T

    @pl.when(block > 0)
    def _():
        up_cols.wait_recv()

    @pl.when(block == 0)
    def _():
        low_cols[...] = jnp.zeros_like(low_cols)

    @pl.when(block < n_mode - 1)
    def _():
        down_cols.wait_recv()

    @pl.when(block == n_mode - 1)
    def _():
        high_cols[...] = jnp.zeros_like(high_cols)

    for c in range(3):
        eig_t[:HALF, c * ATOM_DEV : (c + 1) * ATOM_DEV] = low_cols[c].T
        eig_t[HALF + MODE_DEV :, c * ATOM_DEV : (c + 1) * ATOM_DEV] = high_cols[c].T
    up_rows.wait_recv()
    down_rows.wait_recv()
    project(0)
    project(1)

    @pl.when(block < n_mode - 1)
    def _():
        pl.semaphore_wait(ready.at[1], n_mode - 1 - block)

    lax.fori_loop(1, n_mode - block, send_freq, 0)
    project(2)

    loads[4].wait()
    drain(spectrum.at[pl.ds(1, n_mode - 1), :], freq_recv)
    own_freq = spectrum[pl.ds(0, 1), :]
    columns = spectrum[...].T
    freq_col[:HALF] = jnp.broadcast_to(columns[HALF:, 1:2], (HALF, HALF))
    freq_col[HALF : HALF + MODE_DEV] = jnp.broadcast_to(columns[:, 0:1], (MODE_DEV, HALF))
    freq_col[HALF + MODE_DEV :] = jnp.broadcast_to(
        columns[:HALF, n_mode - 1 : n_mode], (HALF, HALF)
    )
    every = spectrum[...]
    highest = jnp.max(jnp.max(every, axis=1, keepdims=True), axis=0, keepdims=True)
    lowest = jnp.min(jnp.min(every, axis=1, keepdims=True), axis=0, keepdims=True)
    broaden = BROAD * (highest - lowest) / (n_mode * MODE_DEV - 1)

    start = block * MODE_DEV
    first = me * ROWS
    rows = first + iota((ROWS, HALF), 0)
    lanes = iota((ROWS, HALF), 1)
    weights = []
    for h in range(2):
        ours = slice(h * HALF, (h + 1) * HALF)
        mine = own_freq[:, ours]
        lower = band[0:1, ours]
        upper = band[1:2, ours]

        def freq_at(offset):
            return freq_col[pl.ds(pl.multiple_of(offset + first, ROWS), ROWS), :]

        before = freq_at(h * HALF)
        level = freq_at((h + 1) * HALF)
        after = freq_at((h + 2) * HALF)
        base = start + h * HALF + rows
        for partner, ids in (
            (
                jnp.where(rows > lanes, before, after),
                base + jnp.where(rows > lanes, -HALF, HALF),
            ),
            (
                jnp.where(rows == lanes, before, level),
                base + jnp.where(rows == lanes, -HALF, 0),
            ),
        ):
            own_ids = start + h * HALF + lanes
            inside = (ids >= lower) & (ids < upper) & (ids != own_ids)
            detune = mine - partner
            lorentz = broaden / math.pi / (detune * detune + broaden * broaden)
            factor = (mine + partner) ** 2 / (4.0 * mine * partner)
            weights.append((inside, lorentz * factor))

    strength = jnp.zeros((4, ROWS, HALF), F32)
    for k in range(3):
        drain(recv_pair.at[k], pair_recv.at[k])
        total = send_pair[k, me]
        for q in range(n_atom - 1):
            total = total + recv_pair[k, q]
        strength = strength + total * total

    for h in range(2):
        term = 0.0
        for s in range(2):
            inside, weight = weights[2 * h + s]
            term = term + jnp.where(inside, weight * strength[2 * h + s], 0.0)
        send_sum[h : h + 1] = jnp.sum(term, axis=0, keepdims=True)

    def share(q, carry):
        to_atom(send_sum, recv_sum.at[q - 1], q, sum_send, sum_recv).start()
        return carry

    lax.fori_loop(1, n_atom, share, 0)
    freq_two = jnp.concatenate([own_freq[:, :HALF], own_freq[:, HALF:]], axis=0)
    grown = jnp.exp(freq_two)
    capacity = freq_two * freq_two * grown / ((grown - 1.0) * (grown - 1.0))
    prefactor = math.pi / (3.0 * freq_two * freq_two)
    part_total = capacity * prefactor * send_sum[...]
    send_total[...] = part_total[0:1] + part_total[1:2]

    def share_total(t, carry):
        shift = n_mode - 1 - block - t

        def share_to(q, carry):
            pltpu.make_async_remote_copy(
                src_ref=send_total,
                dst_ref=recv_total.at[shift - 1, q],
                send_sem=total_send.at[shift - 1],
                recv_sem=total_recv.at[shift - 1],
                device_id=(lax.rem(me + q, n_atom), block + shift),
                device_id_type=MESH,
            ).start()
            return carry

        return lax.fori_loop(0, n_atom, share_to, carry, unroll=True)

    lax.fori_loop(0, n_mode - 1 - block, share_total, 0)
    drain(recv_sum, sum_recv)
    row_sums = send_sum[...]
    for q in range(n_atom - 1):
        row_sums = row_sums + recv_sum[q]
    diffusivity = prefactor * row_sums
    diff_ref[:, :HALF] = diffusivity[0:1]
    diff_ref[:, HALF:] = diffusivity[1:2]
    running = capacity * diffusivity
    lane_two = iota((2, HALF), 1)
    for step in (1, 2, 4, 8, 16, 32, 64):
        running = running + jnp.where(lane_two >= step, pltpu.roll(running, step, 1), 0.0)
    low_total = running[0:1, HALF - 1 : HALF]
    running = running + jnp.where(iota((2, HALF), 0) == 1, low_total, 0.0)

    def hear_total(t, carry):
        drain(recv_total.at[t], total_recv.at[t])
        return carry

    lax.fori_loop(0, block, hear_total, 0)
    earlier = jnp.sum(
        jnp.sum(jnp.sum(recv_total[...], axis=(0, 1)), axis=0, keepdims=True), axis=1, keepdims=True
    )
    conductivity = (earlier + running) / MODE_DEV
    cond_ref[:, :HALF] = conductivity[0:1]
    cond_ref[:, HALF:] = conductivity[1:2]

    up_rows.wait_send()
    down_rows.wait_send()

    @pl.when(block < n_mode - 1)
    def _():
        up_cols.wait_send()

    @pl.when(block > 0)
    def _():
        down_cols.wait_send()

    drain(spectrum.at[pl.ds(1, n_mode - 1), :], freq_send)
    for k in range(3):
        drain(recv_pair.at[k], pair_send.at[k])
    drain(recv_sum, sum_send)

    def sent_total(t, carry):
        drain(recv_total.at[t], total_send.at[t])
        return carry

    lax.fori_loop(0, n_mode - 1 - block, sent_total, 0)


def body(eigvec, force, bond, nbr, band, freq):
    n_atom, n_mode = lax.axis_size("atom"), lax.axis_size("mode")
    any_spec = pl.BlockSpec(memory_space=pl.ANY)
    vmem_spec = pl.BlockSpec(memory_space=pltpu.VMEM)
    dma = pltpu.SemaphoreType.DMA
    diffusivity, conductivity = pl.pallas_call(
        functools.partial(kernel, n_atom, n_mode),
        out_shape=(
            jax.ShapeDtypeStruct((1, MODE_DEV), F32),
            jax.ShapeDtypeStruct((1, MODE_DEV), F32),
        ),
        in_specs=[any_spec] * 6,
        out_specs=(vmem_spec, vmem_spec),
        scratch_shapes=[
            pltpu.VMEM((3, ATOM_DEV, MODE_DEV), BF16),
            pltpu.VMEM((3, 3, NBR, ATOM_DEV), F32),
            pltpu.VMEM((3, NBR, ATOM_DEV), F32),
            pltpu.VMEM((NBR, ATOM_DEV), jnp.int32),
            pltpu.VMEM((2, MODE_DEV), jnp.int32),
            pltpu.VMEM((n_mode, MODE_DEV), F32),
            pltpu.VMEM((3, RIM, MODE_DEV), BF16),
            pltpu.VMEM((3, RIM, MODE_DEV), BF16),
            pltpu.VMEM((3, ATOM_DEV, HALF), BF16),
            pltpu.VMEM((3, ATOM_DEV, HALF), BF16),
            pltpu.VMEM((ATOM_DEV, NBR), F32),
            pltpu.VMEM((GROUPS, 256, ATOM_DEV), BF16),
            pltpu.VMEM((GROUPS, 27 * GROUP, 256), BF16),
            pltpu.VMEM((9, ATOM_DEV, 3 * ATOM_DEV), BF16),
            pltpu.VMEM((9, ATOM_DEV, 3 * RIM), BF16),
            pltpu.VMEM((3, ATOM_DEV, MODE_DEV), BF16),
            pltpu.VMEM((MODE_DEV + 2 * HALF, 3 * ATOM_DEV), BF16),
            pltpu.VMEM((3, n_atom, 4, ROWS, HALF), F32),
            pltpu.VMEM((3, n_atom - 1, 4, ROWS, HALF), F32),
            pltpu.VMEM((MODE_DEV + 2 * HALF, HALF), F32),
            pltpu.VMEM((2, HALF), F32),
            pltpu.VMEM((n_atom - 1, 2, HALF), F32),
            pltpu.VMEM((1, HALF), F32),
            pltpu.VMEM((n_mode - 1, n_atom, 1, HALF), F32),
            pltpu.VMEM((9, ATOM_DEV, MODE_DEV), F32),
            dma((6,)),
            dma((2,)),
            dma((2,)),
            dma((2,)),
            dma((2,)),
            dma(()),
            dma(()),
            dma((3,)),
            dma((3,)),
            dma(()),
            dma(()),
            dma((n_mode - 1,)),
            dma((n_mode - 1,)),
            pltpu.SemaphoreType.REGULAR((2,)),
        ],
        compiler_params=pltpu.CompilerParams(
            collective_id=0, has_side_effects=True, vmem_limit_bytes=63 * 1024 * 1024
        ),
    )(eigvec, force, bond, nbr, band, freq.reshape(1, MODE_DEV))
    return diffusivity.reshape(MODE_DEV), conductivity.reshape(MODE_DEV)


def solution(mesh):
    in_specs = (
        P(None, "atom", "mode"),
        P(None, None, None, "atom"),
        P(None, None, "atom"),
        P(None, "atom"),
        P(None, "mode"),
        P("mode"),
    )
    out_specs = (P("mode"), P("mode"))
    return jax.shard_map(body, mesh=mesh, in_specs=in_specs, out_specs=out_specs, check_vma=False)
```

```python
import functools
import math

import jax
import jax.numpy as jnp
from jax import lax
from jax.experimental import pallas as pl
from jax.experimental.pallas import tpu as pltpu
from jax.sharding import PartitionSpec as P

ATOM_DEV = 256
MODE_DEV = 256
NBR = 16
RIM = 128
HALF = 128
BROAD = 128
GROUP = 16
GROUPS = ATOM_DEV // GROUP
ROWS = 8
BF16 = jnp.bfloat16
F32 = jnp.float32
MESH = pl.DeviceIdType.MESH


def iota(shape, dim):
    return lax.broadcasted_iota(jnp.int32, shape, dim)


def contract(lhs, rhs, lhs_dim, rhs_dim):
    return lax.dot_general(
        lhs, rhs, (((lhs_dim,), (rhs_dim,)), ((), ())), preferred_element_type=F32
    )


def drain(ref, sem):
    pltpu.make_async_copy(ref, ref, sem).wait()


def kernel(
    n_atom,
    n_mode,
    eig_hbm,
    force_hbm,
    bond_hbm,
    nbr_hbm,
    band_hbm,
    freq_hbm,
    out_ref,
    eig,
    force,
    bond,
    nbr,
    band,
    spectrum,
    low_rows,
    high_rows,
    low_cols,
    high_cols,
    nbr_cols,
    hot,
    spread,
    own_m,
    rim_m,
    flux,
    eig_t,
    send_pair,
    recv_pair,
    freq_col,
    send_sum,
    recv_sum,
    send_total,
    recv_total,
    inner_flux,
    local_sem,
    row_send,
    row_recv,
    col_send,
    col_recv,
    freq_send,
    freq_recv,
    pair_send,
    pair_recv,
    sum_send,
    sum_recv,
    total_send,
    total_recv,
    ready,
):
    me = lax.axis_index("atom")
    block = lax.axis_index("mode")
    atoms = n_atom * ATOM_DEV

    barrier = pltpu.get_barrier_semaphore()

    def greet_atom(q, carry):
        pl.semaphore_signal(
            barrier, inc=1, device_id=(lax.rem(me + q, n_atom), block), device_id_type=MESH
        )
        return carry

    recv_total[...] = jnp.zeros_like(recv_total)
    lax.fori_loop(1, n_atom, greet_atom, 0)

    def beside(shift, action):
        @pl.when(block + shift < n_mode)
        def _():
            action(block + shift)

        @pl.when(block - shift >= 0)
        def _():
            action(block - shift)

    def greet_mode(other):
        pl.semaphore_signal(barrier, inc=1, device_id=(me, other), device_id_type=MESH)

    beside(1, greet_mode)

    loads = [
        pltpu.make_async_copy(nbr_hbm, nbr, local_sem.at[0]),
        pltpu.make_async_copy(bond_hbm, bond, local_sem.at[1]),
        pltpu.make_async_copy(force_hbm, force, local_sem.at[2]),
        pltpu.make_async_copy(eig_hbm, eig, local_sem.at[3]),
        pltpu.make_async_copy(band_hbm, band, local_sem.at[4]),
        pltpu.make_async_copy(freq_hbm, spectrum.at[pl.ds(0, 1), :], local_sem.at[5]),
    ]
    for load in loads:
        load.start()

    lane = iota((ATOM_DEV, 256), 1)
    diagonal = (iota((ATOM_DEV, 256), 0) & (GROUP - 1)) == (lane & (GROUP - 1))
    slot_rows = jnp.where(
        (iota((NBR, 256), 1) >> 4) == iota((NBR, 256), 0), 1.0, 0.0
    ).astype(BF16)

    loads[0].wait()
    atom_ids = iota((NBR, ATOM_DEV), 1)
    offset = ((nbr[...] - me * ATOM_DEV - atom_ids + RIM + atoms) & (atoms - 1)) - RIM
    column = jnp.where(offset == RIM, atom_ids, (atom_ids + offset) & (ATOM_DEV - 1))
    nbr_cols[...] = column.astype(F32).T

    col_ids = iota((GROUP, ATOM_DEV), 1).astype(F32)

    def one_hot(g, carry):
        own_cols = nbr_cols[pl.ds(pl.multiple_of(g * GROUP, GROUP), GROUP), :]
        for n in range(NBR):
            hot[g, n * GROUP : (n + 1) * GROUP, :] = jnp.where(
                own_cols[:, n : n + 1] == col_ids, 1.0, 0.0
            ).astype(BF16)
        return carry

    lax.fori_loop(0, GROUPS, one_hot, 0, unroll=4)

    loads[5].wait()
    loads[3].wait()
    pl.semaphore_wait(
        barrier,
        n_atom - 1 + (block > 0).astype(jnp.int32) + (block < n_mode - 1).astype(jnp.int32),
    )

    def to_atom(src, dst, q, send, recv):
        return pltpu.make_async_remote_copy(
            src_ref=src,
            dst_ref=dst,
            send_sem=send,
            recv_sem=recv,
            device_id=(lax.rem(me + q, n_atom), block),
            device_id_type=MESH,
        )

    def to_mode(src, dst, q, send, recv):
        return pltpu.make_async_remote_copy(
            src_ref=src,
            dst_ref=dst,
            send_sem=send,
            recv_sem=recv,
            device_id=(me, lax.rem(block + q, n_mode)),
            device_id_type=MESH,
        )

    up_rows = to_atom(
        eig.at[:, pl.ds(ATOM_DEV - RIM, RIM), :], low_rows, 1, row_send.at[0], row_recv.at[0]
    )
    down_rows = to_atom(
        eig.at[:, pl.ds(0, RIM), :], high_rows, n_atom - 1, row_send.at[1], row_recv.at[1]
    )
    up_cols = to_mode(
        eig.at[:, :, pl.ds(MODE_DEV - HALF, HALF)], low_cols, 1, col_send.at[0], col_recv.at[0]
    )
    down_cols = to_mode(
        eig.at[:, :, pl.ds(0, HALF)], high_cols, n_mode - 1, col_send.at[1], col_recv.at[1]
    )
    up_rows.start()
    down_rows.start()

    @pl.when(block < n_mode - 1)
    def _():
        up_cols.start()

    @pl.when(block > 0)
    def _():
        down_cols.start()

    @pl.when(block > 0)
    def _():
        pl.semaphore_wait(ready.at[0], 1)

    @pl.when(block < n_mode - 1)
    def _():
        pl.semaphore_signal(
            ready.at[0], inc=1, device_id=(me, block + 1), device_id_type=MESH
        )

    def tell(other, carry):
        pl.semaphore_signal(ready.at[1], inc=1, device_id=(me, other), device_id_type=MESH)
        return carry

    lax.fori_loop(0, block, tell, 0)

    def send_freq(q, carry):
        to_mode(
            spectrum.at[pl.ds(0, 1), :],
            spectrum.at[pl.ds(q, 1), :],
            q,
            freq_send,
            freq_recv,
        ).start()
        return carry

    lax.fori_loop(n_mode - block, n_mode, send_freq, 0)

    loads[1].wait()
    loads[2].wait()

    def spread_out():
        for k in range(3):
            for c in range(3):
                for d in range(3):
                    coupling = (bond[k] * force[c, d]).astype(BF16)
                    wide = jnp.where(diagonal, contract(coupling, slot_rows, 0, 0), 0.0)
                    first = (9 * k + 3 * c + d) * GROUP
                    spread[:, first : first + GROUP, :] = wide.astype(BF16).reshape(
                        GROUPS, GROUP, 256
                    )

    near = iota((GROUP, RIM), 1) - iota((GROUP, RIM), 0)

    def unfold(h, g):
        dense = contract(spread[g], hot[g], 1, 0)
        gap = near - (g - h * (GROUPS // 2)) * GROUP
        below, same = gap < 0, gap == 0
        rows = pl.ds(pl.multiple_of(g * GROUP, GROUP), GROUP)
        for q in range(9):
            for d in range(3):
                first = (3 * q + d) * GROUP
                left = dense[first : first + GROUP, :RIM]
                right = dense[first : first + GROUP, RIM:]
                if h == 0:
                    own_left = jnp.where(same, 0.0, left)
                    own_right = jnp.where(below, right, jnp.where(same, left, 0.0))
                    rim = jnp.where(below, 0.0, right)
                else:
                    own_left = jnp.where(below, 0.0, left)
                    own_right = jnp.where(same, 0.0, right)
                    rim = jnp.where(below, left, jnp.where(same, right, 0.0))
                own_m[q, rows, d * ATOM_DEV : d * ATOM_DEV + RIM] = own_left.astype(BF16)
                own_m[q, rows, d * ATOM_DEV + RIM : (d + 1) * ATOM_DEV] = own_right.astype(BF16)
                rim_m[q, rows, d * RIM : (d + 1) * RIM] = rim.astype(BF16)

    def build():
        for h in range(2):

            def group(g, carry, h=h):
                unfold(h, g)
                return carry

            lax.fori_loop(
                h * (GROUPS // 2), (h + 1) * (GROUPS // 2), group, 0, unroll=True
            )

    row = iota((HALF, HALF), 0)
    col = iota((HALF, HALF), 1)

    def inner_part_of(k):
        inner_flux[3 * k : 3 * k + 3] = contract(
            own_m[3 * k : 3 * k + 3].reshape(3 * ATOM_DEV, 3 * ATOM_DEV),
            eig[...].reshape(3 * ATOM_DEV, MODE_DEV),
            1,
            0,
        ).reshape(3, ATOM_DEV, MODE_DEV)

    def project(k):
        for h, halo in enumerate((low_rows, high_rows)):
            outer = contract(
                rim_m[3 * k : 3 * k + 3, h * RIM : (h + 1) * RIM, :].reshape(3 * RIM, 3 * RIM),
                halo[...].reshape(3 * RIM, MODE_DEV),
                1,
                0,
            ).reshape(3, RIM, MODE_DEV)
            flux[:, h * RIM : (h + 1) * RIM, :] = (
                inner_flux[3 * k : 3 * k + 3, h * RIM : (h + 1) * RIM, :] + outer
            ).astype(BF16)
        pair = contract(eig_t[...], flux[...].reshape(3 * ATOM_DEV, MODE_DEV), 1, 0)
        for h in range(2):
            ours = slice(h * HALF, (h + 1) * HALF)
            before = pair[h * HALF : (h + 1) * HALF, ours]
            level = pair[(h + 1) * HALF : (h + 2) * HALF, ours]
            after = pair[(h + 2) * HALF : (h + 3) * HALF, ours]
            outer = jnp.where(row > col, before, after)
            inner_part = jnp.where(row == col, before, level)
            send_pair[k, :, 2 * h] = outer.reshape(n_atom, ROWS, HALF).astype(BF16)
            send_pair[k, :, 2 * h + 1] = inner_part.reshape(n_atom, ROWS, HALF).astype(BF16)

        def send(q, carry):
            to_atom(
                send_pair.at[k, lax.rem(me + q, n_atom)],
                recv_pair.at[k, q - 1],
                q,
                pair_send.at[k],
                pair_recv.at[k],
            ).start()
            return carry

        lax.fori_loop(1, n_atom, send, 0)

    spread_out()
    build()
    for k in range(3):
        inner_part_of(k)
    for c in range(3):
        eig_t[HALF : HALF + MODE_DEV, c * ATOM_DEV : (c + 1) * ATOM_DEV] = eig[c].T

    @pl.when(block > 0)
    def _():
        up_cols.wait_recv()

    @pl.when(block == 0)
    def _():
        low_cols[...] = jnp.zeros_like(low_cols)

    @pl.when(block < n_mode - 1)
    def _():
        down_cols.wait_recv()

    @pl.when(block == n_mode - 1)
    def _():
        high_cols[...] = jnp.zeros_like(high_cols)

    for c in range(3):
        eig_t[:HALF, c * ATOM_DEV : (c + 1) * ATOM_DEV] = low_cols[c].T
        eig_t[HALF + MODE_DEV :, c * ATOM_DEV : (c + 1) * ATOM_DEV] = high_cols[c].T
    up_rows.wait_recv()
    down_rows.wait_recv()
    project(0)
    project(1)

    @pl.when(block < n_mode - 1)
    def _():
        pl.semaphore_wait(ready.at[1], n_mode - 1 - block)

    lax.fori_loop(1, n_mode - block, send_freq, 0)
    project(2)

    loads[4].wait()
    drain(spectrum.at[pl.ds(1, n_mode - 1), :], freq_recv)
    own_freq = spectrum[pl.ds(0, 1), :]
    columns = spectrum[...].T
    freq_col[:HALF] = jnp.broadcast_to(columns[HALF:, 1:2], (HALF, HALF))
    freq_col[HALF : HALF + MODE_DEV] = jnp.broadcast_to(columns[:, 0:1], (MODE_DEV, HALF))
    freq_col[HALF + MODE_DEV :] = jnp.broadcast_to(
        columns[:HALF, n_mode - 1 : n_mode], (HALF, HALF)
    )
    every = spectrum[...]
    highest = jnp.max(jnp.max(every, axis=1, keepdims=True), axis=0, keepdims=True)
    lowest = jnp.min(jnp.min(every, axis=1, keepdims=True), axis=0, keepdims=True)
    broaden = BROAD * (highest - lowest) / (n_mode * MODE_DEV - 1)

    start = block * MODE_DEV
    first = me * ROWS
    rows = first + iota((ROWS, HALF), 0)
    lanes = iota((ROWS, HALF), 1)
    weights = []
    for h in range(2):
        ours = slice(h * HALF, (h + 1) * HALF)
        mine = own_freq[:, ours]
        lower = band[0:1, ours]
        upper = band[1:2, ours]

        def freq_at(offset):
            return freq_col[pl.ds(pl.multiple_of(offset + first, ROWS), ROWS), :]

        before = freq_at(h * HALF)
        level = freq_at((h + 1) * HALF)
        after = freq_at((h + 2) * HALF)
        base = start + h * HALF + rows
        for partner, ids in (
            (
                jnp.where(rows > lanes, before, after),
                base + jnp.where(rows > lanes, -HALF, HALF),
            ),
            (
                jnp.where(rows == lanes, before, level),
                base + jnp.where(rows == lanes, -HALF, 0),
            ),
        ):
            own_ids = start + h * HALF + lanes
            inside = (ids >= lower) & (ids < upper) & (ids != own_ids)
            detune = mine - partner
            lorentz = broaden / math.pi / (detune * detune + broaden * broaden)
            factor = (mine + partner) ** 2 / (4.0 * mine * partner)
            weights.append((inside, lorentz * factor))

    strength = jnp.zeros((4, ROWS, HALF), F32)
    for k in range(3):
        drain(recv_pair.at[k], pair_recv.at[k])
        total = send_pair[k, me].astype(F32)
        for q in range(n_atom - 1):
            total = total + recv_pair[k, q].astype(F32)
        strength = strength + total * total

    for h in range(2):
        term = 0.0
        for s in range(2):
            inside, weight = weights[2 * h + s]
            term = term + jnp.where(inside, weight * strength[2 * h + s], 0.0)
        send_sum[h : h + 1] = jnp.sum(term, axis=0, keepdims=True)

    def share(q, carry):
        to_atom(send_sum, recv_sum.at[q - 1], q, sum_send, sum_recv).start()
        return carry

    lax.fori_loop(1, n_atom, share, 0)
    freq_two = jnp.concatenate([own_freq[:, :HALF], own_freq[:, HALF:]], axis=0)
    grown = jnp.exp(freq_two)
    capacity = freq_two * freq_two * grown / ((grown - 1.0) * (grown - 1.0))
    prefactor = math.pi / (3.0 * freq_two * freq_two)
    part_total = capacity * prefactor * send_sum[...]
    send_total[...] = part_total[0:1] + part_total[1:2]

    def share_total(t, carry):
        shift = n_mode - 1 - block - t

        def share_to(q, carry):
            pltpu.make_async_remote_copy(
                src_ref=send_total,
                dst_ref=recv_total.at[shift - 1, q],
                send_sem=total_send.at[shift - 1],
                recv_sem=total_recv.at[shift - 1],
                device_id=(lax.rem(me + q, n_atom), block + shift),
                device_id_type=MESH,
            ).start()
            return carry

        return lax.fori_loop(0, n_atom, share_to, carry, unroll=True)

    lax.fori_loop(0, n_mode - 1 - block, share_total, 0)
    drain(recv_sum, sum_recv)
    row_sums = send_sum[...]
    for q in range(n_atom - 1):
        row_sums = row_sums + recv_sum[q]
    diffusivity = prefactor * row_sums
    out_ref[0:1, :HALF] = diffusivity[0:1]
    out_ref[0:1, HALF:] = diffusivity[1:2]
    running = capacity * diffusivity
    lane_two = iota((2, HALF), 1)
    for step in (1, 2, 4, 8, 16, 32, 64):
        running = running + jnp.where(lane_two >= step, pltpu.roll(running, step, 1), 0.0)
    low_total = running[0:1, HALF - 1 : HALF]
    running = running + jnp.where(iota((2, HALF), 0) == 1, low_total, 0.0)

    def hear_total(t, carry):
        drain(recv_total.at[t], total_recv.at[t])
        return carry

    lax.fori_loop(0, block, hear_total, 0)
    earlier = jnp.sum(
        jnp.sum(jnp.sum(recv_total[...], axis=(0, 1)), axis=0, keepdims=True), axis=1, keepdims=True
    )
    conductivity = (earlier + running) / MODE_DEV
    out_ref[1:2, :HALF] = conductivity[0:1]
    out_ref[1:2, HALF:] = conductivity[1:2]

    up_rows.wait_send()
    down_rows.wait_send()

    @pl.when(block < n_mode - 1)
    def _():
        up_cols.wait_send()

    @pl.when(block > 0)
    def _():
        down_cols.wait_send()

    drain(spectrum.at[pl.ds(1, n_mode - 1), :], freq_send)
    for k in range(3):
        drain(recv_pair.at[k], pair_send.at[k])
    drain(recv_sum, sum_send)

    def sent_total(t, carry):
        drain(recv_total.at[t], total_send.at[t])
        return carry

    lax.fori_loop(0, n_mode - 1 - block, sent_total, 0)


def body(eigvec, force, bond, nbr, band, freq):
    n_atom, n_mode = lax.axis_size("atom"), lax.axis_size("mode")
    any_spec = pl.BlockSpec(memory_space=pl.ANY)
    vmem_spec = pl.BlockSpec(memory_space=pltpu.VMEM)
    dma = pltpu.SemaphoreType.DMA
    (both,) = pl.pallas_call(
        functools.partial(kernel, n_atom, n_mode),
        out_shape=(
            jax.ShapeDtypeStruct((2, MODE_DEV), F32),
        ),
        in_specs=[any_spec] * 6,
        out_specs=(vmem_spec,),
        scratch_shapes=[
            pltpu.VMEM((3, ATOM_DEV, MODE_DEV), BF16),
            pltpu.VMEM((3, 3, NBR, ATOM_DEV), F32),
            pltpu.VMEM((3, NBR, ATOM_DEV), F32),
            pltpu.VMEM((NBR, ATOM_DEV), jnp.int32),
            pltpu.VMEM((2, MODE_DEV), jnp.int32),
            pltpu.VMEM((n_mode, MODE_DEV), F32),
            pltpu.VMEM((3, RIM, MODE_DEV), BF16),
            pltpu.VMEM((3, RIM, MODE_DEV), BF16),
            pltpu.VMEM((3, ATOM_DEV, HALF), BF16),
            pltpu.VMEM((3, ATOM_DEV, HALF), BF16),
            pltpu.VMEM((ATOM_DEV, NBR), F32),
            pltpu.VMEM((GROUPS, 256, ATOM_DEV), BF16),
            pltpu.VMEM((GROUPS, 27 * GROUP, 256), BF16),
            pltpu.VMEM((9, ATOM_DEV, 3 * ATOM_DEV), BF16),
            pltpu.VMEM((9, ATOM_DEV, 3 * RIM), BF16),
            pltpu.VMEM((3, ATOM_DEV, MODE_DEV), BF16),
            pltpu.VMEM((MODE_DEV + 2 * HALF, 3 * ATOM_DEV), BF16),
            pltpu.VMEM((3, n_atom, 4, ROWS, HALF), BF16),
            pltpu.VMEM((3, n_atom - 1, 4, ROWS, HALF), BF16),
            pltpu.VMEM((MODE_DEV + 2 * HALF, HALF), F32),
            pltpu.VMEM((2, HALF), F32),
            pltpu.VMEM((n_atom - 1, 2, HALF), F32),
            pltpu.VMEM((1, HALF), F32),
            pltpu.VMEM((n_mode - 1, n_atom, 1, HALF), F32),
            pltpu.VMEM((9, ATOM_DEV, MODE_DEV), F32),
            dma((6,)),
            dma((2,)),
            dma((2,)),
            dma((2,)),
            dma((2,)),
            dma(()),
            dma(()),
            dma((3,)),
            dma((3,)),
            dma(()),
            dma(()),
            dma((n_mode - 1,)),
            dma((n_mode - 1,)),
            pltpu.SemaphoreType.REGULAR((2,)),
        ],
        compiler_params=pltpu.CompilerParams(
            collective_id=0, has_side_effects=True, vmem_limit_bytes=56549376
        ),
    )(eigvec, force, bond, nbr, band, freq.reshape(1, MODE_DEV))
    return both[0], both[1]


def solution(mesh):
    in_specs = (
        P(None, "atom", "mode"),
        P(None, None, None, "atom"),
        P(None, None, "atom"),
        P(None, "atom"),
        P(None, "mode"),
        P("mode"),
    )
    out_specs = (P("mode"), P("mode"))
    return jax.shard_map(body, mesh=mesh, in_specs=in_specs, out_specs=out_specs, check_vma=False)
```

```python
import functools
import math

import jax
import jax.numpy as jnp
from jax import lax
from jax.experimental import pallas as pl
from jax.experimental.pallas import tpu as pltpu
from jax.sharding import PartitionSpec as P

ATOM_DEV = 256
MODE_DEV = 256
NBR = 16
RIM = 128
HALF = 128
BROAD = 128
GROUP = 16
GROUPS = ATOM_DEV // GROUP
ROWS = 8
SIDE = 4
BF16 = jnp.bfloat16
F32 = jnp.float32
MESH = pl.DeviceIdType.MESH


def iota(shape, dim):
    return lax.broadcasted_iota(jnp.int32, shape, dim)


def contract(lhs, rhs, lhs_dim, rhs_dim):
    return lax.dot_general(
        lhs, rhs, (((lhs_dim,), (rhs_dim,)), ((), ())), preferred_element_type=F32
    )


def drain(ref, sem):
    pltpu.make_async_copy(ref, ref, sem).wait()


def kernel(
    n_atom,
    n_mode,
    eig_hbm,
    force_hbm,
    bond_hbm,
    nbr_hbm,
    band_hbm,
    freq_hbm,
    out_ref,
    eig,
    force,
    bond,
    nbr,
    band,
    spectrum,
    low_rows,
    high_rows,
    low_cols,
    high_cols,
    nbr_cols,
    hot,
    spread,
    own_m,
    rim_m,
    flux,
    eig_t,
    send_pair,
    recv_pair,
    freq_col,
    send_sum,
    recv_sum,
    send_total,
    recv_total,
    inner_flux,
    local_sem,
    row_send,
    row_recv,
    col_send,
    col_recv,
    freq_send,
    freq_recv,
    pair_send,
    pair_recv,
    sum_send,
    sum_recv,
    total_send,
    total_recv,
    ready,
):
    me = lax.axis_index("atom")
    block = lax.axis_index("mode")
    atoms = n_atom * ATOM_DEV

    barrier = pltpu.get_barrier_semaphore()

    recv_total[...] = jnp.zeros_like(recv_total)
    x, y = me & (SIDE - 1), me // SIDE

    def across(dx, dy):
        return ((y + dy) & (SIDE - 1)) * SIDE + ((x + dx) & (SIDE - 1))

    adjacent = (across(1, 0), across(SIDE - 1, 0), across(0, 1), across(0, SIDE - 1))
    ring = (lax.rem(me + 1, n_atom), lax.rem(me + n_atom - 1, n_atom))

    def signal(sem, atom, mode):
        pl.semaphore_signal(sem, inc=1, device_id=(atom, mode), device_id_type=MESH)

    for peer in adjacent + ring:
        signal(barrier, peer, block)

    def beside(shift, action):
        @pl.when(block + shift < n_mode)
        def _():
            action(block + shift)

        @pl.when(block - shift >= 0)
        def _():
            action(block - shift)

    beside(1, lambda other: signal(barrier, me, other))

    loads = [
        pltpu.make_async_copy(nbr_hbm, nbr, local_sem.at[0]),
        pltpu.make_async_copy(bond_hbm, bond, local_sem.at[1]),
        pltpu.make_async_copy(force_hbm, force, local_sem.at[2]),
        pltpu.make_async_copy(eig_hbm, eig, local_sem.at[3]),
        pltpu.make_async_copy(band_hbm, band, local_sem.at[4]),
        pltpu.make_async_copy(freq_hbm, spectrum.at[pl.ds(0, 1), :], local_sem.at[5]),
    ]
    for load in loads:
        load.start()

    pl.semaphore_wait(
        barrier,
        6 + (block > 0).astype(jnp.int32) + (block < n_mode - 1).astype(jnp.int32),
    )

    def to_atom(src, dst, q, send, recv):
        return pltpu.make_async_remote_copy(
            src_ref=src,
            dst_ref=dst,
            send_sem=send,
            recv_sem=recv,
            device_id=(lax.rem(me + q, n_atom), block),
            device_id_type=MESH,
        )

    def to_mode(src, dst, q, send, recv):
        return pltpu.make_async_remote_copy(
            src_ref=src,
            dst_ref=dst,
            send_sem=send,
            recv_sem=recv,
            device_id=(me, lax.rem(block + q, n_mode)),
            device_id_type=MESH,
        )

    up_rows = to_atom(
        eig_hbm.at[:, pl.ds(ATOM_DEV - RIM, RIM), :], low_rows, 1, row_send.at[0], row_recv.at[0]
    )
    down_rows = to_atom(
        eig_hbm.at[:, pl.ds(0, RIM), :], high_rows, n_atom - 1, row_send.at[1], row_recv.at[1]
    )
    up_cols = to_mode(
        eig_hbm.at[:, :, pl.ds(MODE_DEV - HALF, HALF)], low_cols, 1, col_send.at[0], col_recv.at[0]
    )
    down_cols = to_mode(
        eig_hbm.at[:, :, pl.ds(0, HALF)], high_cols, n_mode - 1, col_send.at[1], col_recv.at[1]
    )
    up_rows.start()
    down_rows.start()

    @pl.when(block < n_mode - 1)
    def _():
        up_cols.start()

    @pl.when(block > 0)
    def _():
        down_cols.start()

    for peer in adjacent:
        signal(ready.at[2], peer, block)

    def send_freq(q, carry):
        to_mode(
            spectrum.at[pl.ds(0, 1), :],
            spectrum.at[pl.ds(q, 1), :],
            q,
            freq_send,
            freq_recv,
        ).start()
        return carry


    lane = iota((ATOM_DEV, 256), 1)
    diagonal = (iota((ATOM_DEV, 256), 0) & (GROUP - 1)) == (lane & (GROUP - 1))
    slot_rows = jnp.where(
        (iota((NBR, 256), 1) >> 4) == iota((NBR, 256), 0), 1.0, 0.0
    ).astype(BF16)

    loads[0].wait()
    atom_ids = iota((NBR, ATOM_DEV), 1)
    offset = ((nbr[...] - me * ATOM_DEV - atom_ids + RIM + atoms) & (atoms - 1)) - RIM
    column = jnp.where(offset == RIM, atom_ids, (atom_ids + offset) & (ATOM_DEV - 1))
    nbr_cols[...] = column.astype(F32).T

    col_ids = iota((GROUP, ATOM_DEV), 1).astype(F32)

    def one_hot(g, carry):
        own_cols = nbr_cols[pl.ds(pl.multiple_of(g * GROUP, GROUP), GROUP), :]
        for n in range(NBR):
            hot[g, n * GROUP : (n + 1) * GROUP, :] = jnp.where(
                own_cols[:, n : n + 1] == col_ids, 1.0, 0.0
            ).astype(BF16)
        return carry

    lax.fori_loop(0, GROUPS, one_hot, 0, unroll=4)

    pl.semaphore_wait(ready.at[2], len(adjacent))
    signal(ready.at[3], across(2, 0), block)
    signal(ready.at[3], across(0, 2), block)
    loads[5].wait()

    @pl.when(block > 0)
    def _():
        pl.semaphore_wait(ready.at[0], 1)

    @pl.when(block < n_mode - 1)
    def _():
        signal(ready.at[0], me, block + 1)

    def tell(sem):
        def one(other, carry):
            signal(sem, me, other)
            return carry

        lax.fori_loop(0, block, one, 0)

    def hear(sem):
        @pl.when(block < n_mode - 1)
        def _():
            pl.semaphore_wait(sem, n_mode - 1 - block)

    tell(ready.at[4])
    lax.fori_loop(n_mode - block, n_mode, send_freq, 0)
    loads[1].wait()
    loads[2].wait()

    def spread_out():
        for k in range(3):
            for c in range(3):
                for d in range(3):
                    coupling = (bond[k] * force[c, d]).astype(BF16)
                    wide = jnp.where(diagonal, contract(coupling, slot_rows, 0, 0), 0.0)
                    first = (9 * k + 3 * c + d) * GROUP
                    spread[:, first : first + GROUP, :] = wide.astype(BF16).reshape(
                        GROUPS, GROUP, 256
                    )

    near = iota((GROUP, RIM), 1) - iota((GROUP, RIM), 0)

    def unfold(h, g):
        dense = contract(spread[g], hot[g], 1, 0)
        gap = near - (g - h * (GROUPS // 2)) * GROUP
        below, same = gap < 0, gap == 0
        rows = pl.ds(pl.multiple_of(g * GROUP, GROUP), GROUP)
        for q in range(9):
            for d in range(3):
                first = (3 * q + d) * GROUP
                left = dense[first : first + GROUP, :RIM]
                right = dense[first : first + GROUP, RIM:]
                if h == 0:
                    own_left = jnp.where(same, 0.0, left)
                    own_right = jnp.where(below, right, jnp.where(same, left, 0.0))
                    rim = jnp.where(below, 0.0, right)
                else:
                    own_left = jnp.where(below, 0.0, left)
                    own_right = jnp.where(same, 0.0, right)
                    rim = jnp.where(below, left, jnp.where(same, right, 0.0))
                own_m[q, rows, d * ATOM_DEV : d * ATOM_DEV + RIM] = own_left.astype(BF16)
                own_m[q, rows, d * ATOM_DEV + RIM : (d + 1) * ATOM_DEV] = own_right.astype(BF16)
                rim_m[q, rows, d * RIM : (d + 1) * RIM] = rim.astype(BF16)

    def build():
        for h in range(2):

            def group(g, carry, h=h):
                unfold(h, g)
                return carry

            lax.fori_loop(
                h * (GROUPS // 2), (h + 1) * (GROUPS // 2), group, 0, unroll=True
            )

    row = iota((HALF, HALF), 0)
    col = iota((HALF, HALF), 1)

    def inner_part_of(k):
        inner_flux[3 * k : 3 * k + 3] = contract(
            own_m[3 * k : 3 * k + 3].reshape(3 * ATOM_DEV, 3 * ATOM_DEV),
            eig[...].reshape(3 * ATOM_DEV, MODE_DEV),
            1,
            0,
        ).reshape(3, ATOM_DEV, MODE_DEV)

    def project(k):
        for h, halo in enumerate((low_rows, high_rows)):
            outer = contract(
                rim_m[3 * k : 3 * k + 3, h * RIM : (h + 1) * RIM, :].reshape(3 * RIM, 3 * RIM),
                halo[...].reshape(3 * RIM, MODE_DEV),
                1,
                0,
            ).reshape(3, RIM, MODE_DEV)
            flux[:, h * RIM : (h + 1) * RIM, :] = (
                inner_flux[3 * k : 3 * k + 3, h * RIM : (h + 1) * RIM, :] + outer
            ).astype(BF16)
        pair = contract(eig_t[...], flux[...].reshape(3 * ATOM_DEV, MODE_DEV), 1, 0)
        for h in range(2):
            ours = slice(h * HALF, (h + 1) * HALF)
            before = pair[h * HALF : (h + 1) * HALF, ours]
            level = pair[(h + 1) * HALF : (h + 2) * HALF, ours]
            after = pair[(h + 2) * HALF : (h + 3) * HALF, ours]
            outer = jnp.where(row > col, before, after)
            inner_part = jnp.where(row == col, before, level)
            send_pair[k, :, 2 * h] = outer.reshape(n_atom, ROWS, HALF).astype(BF16)
            send_pair[k, :, 2 * h + 1] = inner_part.reshape(n_atom, ROWS, HALF).astype(BF16)

        def send(q, carry):
            to_atom(
                send_pair.at[k, lax.rem(me + q, n_atom)],
                recv_pair.at[k, q - 1],
                q,
                pair_send.at[k],
                pair_recv.at[k],
            ).start()
            return carry

        lax.fori_loop(1, n_atom, send, 0)

    spread_out()
    build()
    loads[3].wait()
    for k in range(3):
        inner_part_of(k)
    for c in range(3):
        eig_t[HALF : HALF + MODE_DEV, c * ATOM_DEV : (c + 1) * ATOM_DEV] = eig[c].T

    @pl.when(block > 0)
    def _():
        up_cols.wait_recv()

    @pl.when(block == 0)
    def _():
        low_cols[...] = jnp.zeros_like(low_cols)

    @pl.when(block < n_mode - 1)
    def _():
        down_cols.wait_recv()

    @pl.when(block == n_mode - 1)
    def _():
        high_cols[...] = jnp.zeros_like(high_cols)

    for c in range(3):
        eig_t[:HALF, c * ATOM_DEV : (c + 1) * ATOM_DEV] = low_cols[c].T
        eig_t[HALF + MODE_DEV :, c * ATOM_DEV : (c + 1) * ATOM_DEV] = high_cols[c].T
    up_rows.wait_recv()
    down_rows.wait_recv()
    pl.semaphore_wait(ready.at[3], 2)
    tell(ready.at[1])
    project(0)
    project(1)
    hear(ready.at[4])
    lax.fori_loop(1, n_mode - block, send_freq, 0)
    project(2)

    loads[4].wait()
    drain(spectrum.at[pl.ds(1, n_mode - 1), :], freq_recv)
    own_freq = spectrum[pl.ds(0, 1), :]
    columns = spectrum[...].T
    freq_col[:HALF] = jnp.broadcast_to(columns[HALF:, 1:2], (HALF, HALF))
    freq_col[HALF : HALF + MODE_DEV] = jnp.broadcast_to(columns[:, 0:1], (MODE_DEV, HALF))
    freq_col[HALF + MODE_DEV :] = jnp.broadcast_to(
        columns[:HALF, n_mode - 1 : n_mode], (HALF, HALF)
    )
    every = spectrum[...]
    highest = jnp.max(jnp.max(every, axis=1, keepdims=True), axis=0, keepdims=True)
    lowest = jnp.min(jnp.min(every, axis=1, keepdims=True), axis=0, keepdims=True)
    broaden = BROAD * (highest - lowest) / (n_mode * MODE_DEV - 1)

    start = block * MODE_DEV
    first = me * ROWS
    rows = first + iota((ROWS, HALF), 0)
    lanes = iota((ROWS, HALF), 1)
    weights = []
    for h in range(2):
        ours = slice(h * HALF, (h + 1) * HALF)
        mine = own_freq[:, ours]
        lower = band[0:1, ours]
        upper = band[1:2, ours]

        def freq_at(offset):
            return freq_col[pl.ds(pl.multiple_of(offset + first, ROWS), ROWS), :]

        before = freq_at(h * HALF)
        level = freq_at((h + 1) * HALF)
        after = freq_at((h + 2) * HALF)
        base = start + h * HALF + rows
        for partner, ids in (
            (
                jnp.where(rows > lanes, before, after),
                base + jnp.where(rows > lanes, -HALF, HALF),
            ),
            (
                jnp.where(rows == lanes, before, level),
                base + jnp.where(rows == lanes, -HALF, 0),
            ),
        ):
            own_ids = start + h * HALF + lanes
            inside = (ids >= lower) & (ids < upper) & (ids != own_ids)
            detune = mine - partner
            lorentz = broaden / math.pi / (detune * detune + broaden * broaden)
            factor = (mine + partner) ** 2 / (4.0 * mine * partner)
            weights.append((inside, lorentz * factor))

    strength = jnp.zeros((4, ROWS, HALF), F32)
    for k in range(3):
        drain(recv_pair.at[k], pair_recv.at[k])
        total = send_pair[k, me].astype(F32)
        for q in range(n_atom - 1):
            total = total + recv_pair[k, q].astype(F32)
        strength = strength + total * total

    for h in range(2):
        term = 0.0
        for s in range(2):
            inside, weight = weights[2 * h + s]
            term = term + jnp.where(inside, weight * strength[2 * h + s], 0.0)
        send_sum[h : h + 1] = jnp.sum(term, axis=0, keepdims=True)

    def share(q, carry):
        to_atom(send_sum, recv_sum.at[q - 1], q, sum_send, sum_recv).start()
        return carry

    lax.fori_loop(1, n_atom, share, 0)
    freq_two = jnp.concatenate([own_freq[:, :HALF], own_freq[:, HALF:]], axis=0)
    grown = jnp.exp(freq_two)
    capacity = freq_two * freq_two * grown / ((grown - 1.0) * (grown - 1.0))
    prefactor = math.pi / (3.0 * freq_two * freq_two)
    part_total = capacity * prefactor * send_sum[...]
    send_total[...] = part_total[0:1] + part_total[1:2]

    def share_total(t, carry):
        shift = n_mode - 1 - block - t

        def share_to(q, carry):
            pltpu.make_async_remote_copy(
                src_ref=send_total,
                dst_ref=recv_total.at[shift - 1, q],
                send_sem=total_send.at[shift - 1],
                recv_sem=total_recv.at[shift - 1],
                device_id=(lax.rem(me + q, n_atom), block + shift),
                device_id_type=MESH,
            ).start()
            return carry

        return lax.fori_loop(0, n_atom, share_to, carry, unroll=True)

    hear(ready.at[1])
    lax.fori_loop(0, n_mode - 1 - block, share_total, 0)
    drain(recv_sum, sum_recv)
    row_sums = send_sum[...]
    for q in range(n_atom - 1):
        row_sums = row_sums + recv_sum[q]
    diffusivity = prefactor * row_sums
    out_ref[0:1, :HALF] = diffusivity[0:1]
    out_ref[0:1, HALF:] = diffusivity[1:2]
    running = capacity * diffusivity
    lane_two = iota((2, HALF), 1)
    for step in (1, 2, 4, 8, 16, 32, 64):
        running = running + jnp.where(lane_two >= step, pltpu.roll(running, step, 1), 0.0)
    low_total = running[0:1, HALF - 1 : HALF]
    running = running + jnp.where(iota((2, HALF), 0) == 1, low_total, 0.0)

    def hear_total(t, carry):
        drain(recv_total.at[t], total_recv.at[t])
        return carry

    lax.fori_loop(0, block, hear_total, 0)
    earlier = jnp.sum(
        jnp.sum(jnp.sum(recv_total[...], axis=(0, 1)), axis=0, keepdims=True), axis=1, keepdims=True
    )
    conductivity = (earlier + running) / MODE_DEV
    out_ref[1:2, :HALF] = conductivity[0:1]
    out_ref[1:2, HALF:] = conductivity[1:2]

    up_rows.wait_send()
    down_rows.wait_send()

    @pl.when(block < n_mode - 1)
    def _():
        up_cols.wait_send()

    @pl.when(block > 0)
    def _():
        down_cols.wait_send()

    drain(spectrum.at[pl.ds(1, n_mode - 1), :], freq_send)
    for k in range(3):
        drain(recv_pair.at[k], pair_send.at[k])
    drain(recv_sum, sum_send)

    def sent_total(t, carry):
        drain(recv_total.at[t], total_send.at[t])
        return carry

    lax.fori_loop(0, n_mode - 1 - block, sent_total, 0)


def body(eigvec, force, bond, nbr, band, freq):
    n_atom, n_mode = lax.axis_size("atom"), lax.axis_size("mode")
    any_spec = pl.BlockSpec(memory_space=pl.ANY)
    vmem_spec = pl.BlockSpec(memory_space=pltpu.VMEM)
    dma = pltpu.SemaphoreType.DMA
    (both,) = pl.pallas_call(
        functools.partial(kernel, n_atom, n_mode),
        out_shape=(
            jax.ShapeDtypeStruct((2, MODE_DEV), F32),
        ),
        in_specs=[any_spec] * 6,
        out_specs=(vmem_spec,),
        scratch_shapes=[
            pltpu.VMEM((3, ATOM_DEV, MODE_DEV), BF16),
            pltpu.VMEM((3, 3, NBR, ATOM_DEV), F32),
            pltpu.VMEM((3, NBR, ATOM_DEV), F32),
            pltpu.VMEM((NBR, ATOM_DEV), jnp.int32),
            pltpu.VMEM((2, MODE_DEV), jnp.int32),
            pltpu.VMEM((n_mode, MODE_DEV), F32),
            pltpu.VMEM((3, RIM, MODE_DEV), BF16),
            pltpu.VMEM((3, RIM, MODE_DEV), BF16),
            pltpu.VMEM((3, ATOM_DEV, HALF), BF16),
            pltpu.VMEM((3, ATOM_DEV, HALF), BF16),
            pltpu.VMEM((ATOM_DEV, NBR), F32),
            pltpu.VMEM((GROUPS, 256, ATOM_DEV), BF16),
            pltpu.VMEM((GROUPS, 27 * GROUP, 256), BF16),
            pltpu.VMEM((9, ATOM_DEV, 3 * ATOM_DEV), BF16),
            pltpu.VMEM((9, ATOM_DEV, 3 * RIM), BF16),
            pltpu.VMEM((3, ATOM_DEV, MODE_DEV), BF16),
            pltpu.VMEM((MODE_DEV + 2 * HALF, 3 * ATOM_DEV), BF16),
            pltpu.VMEM((3, n_atom, 4, ROWS, HALF), BF16),
            pltpu.VMEM((3, n_atom - 1, 4, ROWS, HALF), BF16),
            pltpu.VMEM((MODE_DEV + 2 * HALF, HALF), F32),
            pltpu.VMEM((2, HALF), F32),
            pltpu.VMEM((n_atom - 1, 2, HALF), F32),
            pltpu.VMEM((1, HALF), F32),
            pltpu.VMEM((n_mode - 1, n_atom, 1, HALF), F32),
            pltpu.VMEM((9, ATOM_DEV, MODE_DEV), F32),
            dma((6,)),
            dma((2,)),
            dma((2,)),
            dma((2,)),
            dma((2,)),
            dma(()),
            dma(()),
            dma((3,)),
            dma((3,)),
            dma(()),
            dma(()),
            dma((n_mode - 1,)),
            dma((n_mode - 1,)),
            pltpu.SemaphoreType.REGULAR((5,)),
        ],
        compiler_params=pltpu.CompilerParams(
            collective_id=0, has_side_effects=True, vmem_limit_bytes=56549376
        ),
    )(eigvec, force, bond, nbr, band, freq.reshape(1, MODE_DEV))
    return both[0], both[1]


def solution(mesh):
    in_specs = (
        P(None, "atom", "mode"),
        P(None, None, None, "atom"),
        P(None, None, "atom"),
        P(None, "atom"),
        P(None, "mode"),
        P("mode"),
    )
    out_specs = (P("mode"), P("mode"))
    return jax.shard_map(body, mesh=mesh, in_specs=in_specs, out_specs=out_specs, check_vma=False)
```

```python
import functools
import math

import jax
import jax.numpy as jnp
from jax import lax
from jax.experimental import pallas as pl
from jax.experimental.pallas import tpu as pltpu
from jax.sharding import PartitionSpec as P

ATOM_DEV = 256
MODE_DEV = 256
NBR = 16
RIM = 128
HALF = 128
BROAD = 128
GROUP = 16
GROUPS = ATOM_DEV // GROUP
ROWS = 8
SIDE = 4
FAR_FIRST = sorted(
    ((dx, dy) for dx in range(SIDE) for dy in range(SIDE) if dx or dy),
    key=lambda step: -sum(min(part, SIDE - part) for part in step),
)
BF16 = jnp.bfloat16
F32 = jnp.float32
MESH = pl.DeviceIdType.MESH


def iota(shape, dim):
    return lax.broadcasted_iota(jnp.int32, shape, dim)


def contract(lhs, rhs, lhs_dim, rhs_dim):
    return lax.dot_general(
        lhs, rhs, (((lhs_dim,), (rhs_dim,)), ((), ())), preferred_element_type=F32
    )


def drain(ref, sem):
    pltpu.make_async_copy(ref, ref, sem).wait()


def kernel(
    n_atom,
    n_mode,
    eig_hbm,
    force_hbm,
    bond_hbm,
    nbr_hbm,
    band_hbm,
    freq_hbm,
    out_ref,
    eig,
    force,
    bond,
    nbr,
    band,
    spectrum,
    low_rows,
    high_rows,
    low_cols,
    high_cols,
    nbr_cols,
    hot,
    spread,
    own_m,
    rim_m,
    flux,
    eig_t,
    send_pair,
    recv_pair,
    freq_col,
    send_sum,
    recv_sum,
    send_total,
    recv_total,
    inner_flux,
    local_sem,
    row_send,
    row_recv,
    col_send,
    col_recv,
    freq_send,
    freq_recv,
    pair_send,
    pair_recv,
    sum_send,
    sum_recv,
    total_send,
    total_recv,
    ready,
):
    me = lax.axis_index("atom")
    block = lax.axis_index("mode")
    atoms = n_atom * ATOM_DEV

    barrier = pltpu.get_barrier_semaphore()

    recv_total[...] = jnp.zeros_like(recv_total)
    x, y = me & (SIDE - 1), me // SIDE

    def across(dx, dy):
        return ((y + dy) & (SIDE - 1)) * SIDE + ((x + dx) & (SIDE - 1))

    adjacent = (across(1, 0), across(SIDE - 1, 0), across(0, 1), across(0, SIDE - 1))
    ring = (lax.rem(me + 1, n_atom), lax.rem(me + n_atom - 1, n_atom))

    def signal(sem, atom, mode):
        pl.semaphore_signal(sem, inc=1, device_id=(atom, mode), device_id_type=MESH)

    for peer in adjacent + ring:
        signal(barrier, peer, block)

    def beside(shift, action):
        @pl.when(block + shift < n_mode)
        def _():
            action(block + shift)

        @pl.when(block - shift >= 0)
        def _():
            action(block - shift)

    beside(1, lambda other: signal(barrier, me, other))

    loads = [
        pltpu.make_async_copy(nbr_hbm, nbr, local_sem.at[0]),
        pltpu.make_async_copy(bond_hbm, bond, local_sem.at[1]),
        pltpu.make_async_copy(force_hbm, force, local_sem.at[2]),
        pltpu.make_async_copy(eig_hbm, eig, local_sem.at[3]),
        pltpu.make_async_copy(band_hbm, band, local_sem.at[4]),
        pltpu.make_async_copy(freq_hbm, spectrum.at[pl.ds(0, 1), :], local_sem.at[5]),
    ]
    for load in loads:
        load.start()

    pl.semaphore_wait(
        barrier,
        6 + (block > 0).astype(jnp.int32) + (block < n_mode - 1).astype(jnp.int32),
    )

    def to_atom(src, dst, q, send, recv):
        return pltpu.make_async_remote_copy(
            src_ref=src,
            dst_ref=dst,
            send_sem=send,
            recv_sem=recv,
            device_id=(lax.rem(me + q, n_atom), block),
            device_id_type=MESH,
        )

    def to_mode(src, dst, q, send, recv):
        return pltpu.make_async_remote_copy(
            src_ref=src,
            dst_ref=dst,
            send_sem=send,
            recv_sem=recv,
            device_id=(me, lax.rem(block + q, n_mode)),
            device_id_type=MESH,
        )

    def rim_copies(h):
        cols = pl.ds(h * HALF, HALF)
        up = to_atom(
            eig_hbm.at[:, pl.ds(ATOM_DEV - RIM, RIM), cols],
            low_rows.at[h],
            1,
            row_send.at[h, 0],
            row_recv.at[h, 0],
        )
        down = to_atom(
            eig_hbm.at[:, pl.ds(0, RIM), cols],
            high_rows.at[h],
            n_atom - 1,
            row_send.at[h, 1],
            row_recv.at[h, 1],
        )
        return up, down

    rims = rim_copies(0) + rim_copies(1)
    up_cols = to_mode(
        eig_hbm.at[:, :, pl.ds(MODE_DEV - HALF, HALF)], low_cols, 1, col_send.at[0], col_recv.at[0]
    )
    down_cols = to_mode(
        eig_hbm.at[:, :, pl.ds(0, HALF)], high_cols, n_mode - 1, col_send.at[1], col_recv.at[1]
    )
    for rim in rims:
        rim.start()

    @pl.when(block < n_mode - 1)
    def _():
        up_cols.start()

    @pl.when(block > 0)
    def _():
        down_cols.start()

    for peer in adjacent:
        signal(ready.at[2], peer, block)

    def send_freq(q, carry):
        to_mode(
            spectrum.at[pl.ds(0, 1), :],
            spectrum.at[pl.ds(q, 1), :],
            q,
            freq_send,
            freq_recv,
        ).start()
        return carry


    lane = iota((ATOM_DEV, 256), 1)
    diagonal = (iota((ATOM_DEV, 256), 0) & (GROUP - 1)) == (lane & (GROUP - 1))
    slot_rows = jnp.where(
        (iota((NBR, 256), 1) >> 4) == iota((NBR, 256), 0), 1.0, 0.0
    ).astype(BF16)

    loads[0].wait()
    atom_ids = iota((NBR, ATOM_DEV), 1)
    offset = ((nbr[...] - me * ATOM_DEV - atom_ids + RIM + atoms) & (atoms - 1)) - RIM
    column = jnp.where(offset == RIM, atom_ids, (atom_ids + offset) & (ATOM_DEV - 1))
    nbr_cols[...] = column.astype(F32).T

    col_ids = iota((GROUP, ATOM_DEV), 1).astype(F32)

    def one_hot(g, carry):
        own_cols = nbr_cols[pl.ds(pl.multiple_of(g * GROUP, GROUP), GROUP), :]
        for n in range(NBR):
            hot[g, n * GROUP : (n + 1) * GROUP, :] = jnp.where(
                own_cols[:, n : n + 1] == col_ids, 1.0, 0.0
            ).astype(BF16)
        return carry

    lax.fori_loop(0, GROUPS, one_hot, 0, unroll=4)

    pl.semaphore_wait(ready.at[2], len(adjacent))
    signal(ready.at[3], across(2, 0), block)
    signal(ready.at[3], across(0, 2), block)
    loads[5].wait()

    @pl.when(block > 0)
    def _():
        pl.semaphore_wait(ready.at[0], 1)

    @pl.when(block < n_mode - 1)
    def _():
        signal(ready.at[0], me, block + 1)

    def tell(sem):
        def one(other, carry):
            signal(sem, me, other)
            return carry

        lax.fori_loop(0, block, one, 0)

    def hear(sem):
        @pl.when(block < n_mode - 1)
        def _():
            pl.semaphore_wait(sem, n_mode - 1 - block)

    tell(ready.at[4])
    lax.fori_loop(n_mode - block, n_mode, send_freq, 0)
    loads[1].wait()
    loads[2].wait()

    def spread_out():
        for k in range(3):
            for c in range(3):
                for d in range(3):
                    coupling = (bond[k] * force[c, d]).astype(BF16)
                    wide = jnp.where(diagonal, contract(coupling, slot_rows, 0, 0), 0.0)
                    first = (9 * k + 3 * c + d) * GROUP
                    spread[:, first : first + GROUP, :] = wide.astype(BF16).reshape(
                        GROUPS, GROUP, 256
                    )

    near = iota((GROUP, RIM), 1) - iota((GROUP, RIM), 0)

    def unfold(h, g):
        dense = contract(spread[g], hot[g], 1, 0)
        gap = near - (g - h * (GROUPS // 2)) * GROUP
        below, same = gap < 0, gap == 0
        rows = pl.ds(pl.multiple_of(g * GROUP, GROUP), GROUP)
        for q in range(9):
            for d in range(3):
                first = (3 * q + d) * GROUP
                left = dense[first : first + GROUP, :RIM]
                right = dense[first : first + GROUP, RIM:]
                if h == 0:
                    own_left = jnp.where(same, 0.0, left)
                    own_right = jnp.where(below, right, jnp.where(same, left, 0.0))
                    rim = jnp.where(below, 0.0, right)
                else:
                    own_left = jnp.where(below, 0.0, left)
                    own_right = jnp.where(same, 0.0, right)
                    rim = jnp.where(below, left, jnp.where(same, right, 0.0))
                own_m[q, rows, d * ATOM_DEV : d * ATOM_DEV + RIM] = own_left.astype(BF16)
                own_m[q, rows, d * ATOM_DEV + RIM : (d + 1) * ATOM_DEV] = own_right.astype(BF16)
                rim_m[q, rows, d * RIM : (d + 1) * RIM] = rim.astype(BF16)

    def build():
        for h in range(2):

            def group(g, carry, h=h):
                unfold(h, g)
                return carry

            lax.fori_loop(
                h * (GROUPS // 2), (h + 1) * (GROUPS // 2), group, 0, unroll=True
            )

    row = iota((HALF, HALF), 0)
    col = iota((HALF, HALF), 1)

    def inner_part_of(k):
        inner_flux[3 * k : 3 * k + 3] = contract(
            own_m[3 * k : 3 * k + 3].reshape(3 * ATOM_DEV, 3 * ATOM_DEV),
            eig[...].reshape(3 * ATOM_DEV, MODE_DEV),
            1,
            0,
        ).reshape(3, ATOM_DEV, MODE_DEV)

    def project(h, k):
        ours = slice(h * HALF, (h + 1) * HALF)
        for side, halo in enumerate((low_rows, high_rows)):
            rows = slice(side * RIM, (side + 1) * RIM)
            outer = contract(
                rim_m[3 * k : 3 * k + 3, rows, :].reshape(3 * RIM, 3 * RIM),
                halo[h].reshape(3 * RIM, HALF),
                1,
                0,
            ).reshape(3, RIM, HALF)
            flux[h, :, rows, :] = (inner_flux[3 * k : 3 * k + 3, rows, ours] + outer).astype(BF16)
        pair = contract(
            eig_t[h * HALF : (h + 3) * HALF], flux[h].reshape(3 * ATOM_DEV, HALF), 1, 0
        )
        before, level, after = (pair[s * HALF : (s + 1) * HALF] for s in range(3))
        outer = jnp.where(row > col, before, after)
        inner_part = jnp.where(row == col, before, level)
        send_pair[h, :, k, 0] = outer.reshape(n_atom, ROWS, HALF).astype(BF16)
        send_pair[h, :, k, 1] = inner_part.reshape(n_atom, ROWS, HALF).astype(BF16)

    def scatter(h):
        for slot, (dx, dy) in enumerate(FAR_FIRST):
            peer = across(dx, dy)
            pltpu.make_async_remote_copy(
                src_ref=send_pair.at[h, peer],
                dst_ref=recv_pair.at[h, slot],
                send_sem=pair_send.at[h],
                recv_sem=pair_recv.at[h],
                device_id=(peer, block),
                device_id_type=MESH,
            ).start()

    spread_out()
    build()
    loads[3].wait()
    for k in range(3):
        inner_part_of(k)
    for c in range(3):
        eig_t[HALF : HALF + MODE_DEV, c * ATOM_DEV : (c + 1) * ATOM_DEV] = eig[c].T

    @pl.when(block > 0)
    def _():
        up_cols.wait_recv()

    @pl.when(block == 0)
    def _():
        low_cols[...] = jnp.zeros_like(low_cols)

    @pl.when(block < n_mode - 1)
    def _():
        down_cols.wait_recv()

    @pl.when(block == n_mode - 1)
    def _():
        high_cols[...] = jnp.zeros_like(high_cols)

    for c in range(3):
        eig_t[:HALF, c * ATOM_DEV : (c + 1) * ATOM_DEV] = low_cols[c].T
        eig_t[HALF + MODE_DEV :, c * ATOM_DEV : (c + 1) * ATOM_DEV] = high_cols[c].T
    for rim in rims[:2]:
        rim.wait_recv()
    pl.semaphore_wait(ready.at[3], 2)
    tell(ready.at[1])
    for k in range(3):
        project(0, k)
    scatter(0)
    for rim in rims[2:]:
        rim.wait_recv()
    for k in range(3):
        project(1, k)
    scatter(1)
    hear(ready.at[4])
    lax.fori_loop(1, n_mode - block, send_freq, 0)

    loads[4].wait()
    drain(spectrum.at[pl.ds(1, n_mode - 1), :], freq_recv)
    own_freq = spectrum[pl.ds(0, 1), :]
    columns = spectrum[...].T
    freq_col[:HALF] = jnp.broadcast_to(columns[HALF:, 1:2], (HALF, HALF))
    freq_col[HALF : HALF + MODE_DEV] = jnp.broadcast_to(columns[:, 0:1], (MODE_DEV, HALF))
    freq_col[HALF + MODE_DEV :] = jnp.broadcast_to(
        columns[:HALF, n_mode - 1 : n_mode], (HALF, HALF)
    )
    every = spectrum[...]
    highest = jnp.max(jnp.max(every, axis=1, keepdims=True), axis=0, keepdims=True)
    lowest = jnp.min(jnp.min(every, axis=1, keepdims=True), axis=0, keepdims=True)
    broaden = BROAD * (highest - lowest) / (n_mode * MODE_DEV - 1)

    start = block * MODE_DEV
    first = me * ROWS
    rows = first + iota((ROWS, HALF), 0)
    lanes = iota((ROWS, HALF), 1)
    weights = []
    for h in range(2):
        ours = slice(h * HALF, (h + 1) * HALF)
        mine = own_freq[:, ours]
        lower = band[0:1, ours]
        upper = band[1:2, ours]

        def freq_at(offset):
            return freq_col[pl.ds(pl.multiple_of(offset + first, ROWS), ROWS), :]

        before = freq_at(h * HALF)
        level = freq_at((h + 1) * HALF)
        after = freq_at((h + 2) * HALF)
        base = start + h * HALF + rows
        for partner, ids in (
            (
                jnp.where(rows > lanes, before, after),
                base + jnp.where(rows > lanes, -HALF, HALF),
            ),
            (
                jnp.where(rows == lanes, before, level),
                base + jnp.where(rows == lanes, -HALF, 0),
            ),
        ):
            own_ids = start + h * HALF + lanes
            inside = (ids >= lower) & (ids < upper) & (ids != own_ids)
            detune = mine - partner
            lorentz = broaden / math.pi / (detune * detune + broaden * broaden)
            factor = (mine + partner) ** 2 / (4.0 * mine * partner)
            weights.append((inside, lorentz * factor))

    for h in range(2):
        drain(recv_pair.at[h], pair_recv.at[h])
        total = send_pair[h, me].astype(F32)
        for q in range(n_atom - 1):
            total = total + recv_pair[h, q].astype(F32)
        strength = jnp.sum(total * total, axis=0)
        term = 0.0
        for s in range(2):
            inside, weight = weights[2 * h + s]
            term = term + jnp.where(inside, weight * strength[s], 0.0)
        send_sum[h : h + 1] = jnp.sum(term, axis=0, keepdims=True)

    for slot, (dx, dy) in enumerate(FAR_FIRST):
        pltpu.make_async_remote_copy(
            src_ref=send_sum,
            dst_ref=recv_sum.at[slot],
            send_sem=sum_send,
            recv_sem=sum_recv,
            device_id=(across(dx, dy), block),
            device_id_type=MESH,
        ).start()
    freq_two = jnp.concatenate([own_freq[:, :HALF], own_freq[:, HALF:]], axis=0)
    grown = jnp.exp(freq_two)
    capacity = freq_two * freq_two * grown / ((grown - 1.0) * (grown - 1.0))
    prefactor = math.pi / (3.0 * freq_two * freq_two)
    part_total = capacity * prefactor * send_sum[...]
    send_total[...] = part_total[0:1] + part_total[1:2]

    def share_total(shift):
        for slot, (dx, dy) in enumerate(FAR_FIRST + [(0, 0)]):
            pltpu.make_async_remote_copy(
                src_ref=send_total,
                dst_ref=recv_total.at[shift - 1, slot],
                send_sem=total_send.at[shift - 1],
                recv_sem=total_recv.at[shift - 1],
                device_id=(across(dx, dy), block + shift),
                device_id_type=MESH,
            ).start()

    hear(ready.at[1])
    for shift in range(n_mode - 1, 0, -1):
        pl.when(block + shift < n_mode)(functools.partial(share_total, shift))
    drain(recv_sum, sum_recv)
    row_sums = send_sum[...]
    for q in range(n_atom - 1):
        row_sums = row_sums + recv_sum[q]
    diffusivity = prefactor * row_sums
    out_ref[0:1, :HALF] = diffusivity[0:1]
    out_ref[0:1, HALF:] = diffusivity[1:2]
    running = capacity * diffusivity
    lane_two = iota((2, HALF), 1)
    for step in (1, 2, 4, 8, 16, 32, 64):
        running = running + jnp.where(lane_two >= step, pltpu.roll(running, step, 1), 0.0)
    low_total = running[0:1, HALF - 1 : HALF]
    running = running + jnp.where(iota((2, HALF), 0) == 1, low_total, 0.0)

    def hear_total(t, carry):
        drain(recv_total.at[t], total_recv.at[t])
        return carry

    lax.fori_loop(0, block, hear_total, 0)
    earlier = jnp.sum(
        jnp.sum(jnp.sum(recv_total[...], axis=(0, 1)), axis=0, keepdims=True), axis=1, keepdims=True
    )
    conductivity = (earlier + running) / MODE_DEV
    out_ref[1:2, :HALF] = conductivity[0:1]
    out_ref[1:2, HALF:] = conductivity[1:2]

    for rim in rims:
        rim.wait_send()

    @pl.when(block < n_mode - 1)
    def _():
        up_cols.wait_send()

    @pl.when(block > 0)
    def _():
        down_cols.wait_send()

    drain(spectrum.at[pl.ds(1, n_mode - 1), :], freq_send)
    for h in range(2):
        drain(recv_pair.at[h], pair_send.at[h])
    drain(recv_sum, sum_send)

    def sent_total(t, carry):
        drain(recv_total.at[t], total_send.at[t])
        return carry

    lax.fori_loop(0, n_mode - 1 - block, sent_total, 0)


def body(eigvec, force, bond, nbr, band, freq):
    n_atom, n_mode = lax.axis_size("atom"), lax.axis_size("mode")
    operands = (eigvec, force, bond, nbr, band, freq.reshape(1, MODE_DEV))
    any_spec = pl.BlockSpec(memory_space=pl.ANY)
    vmem_spec = pl.BlockSpec(memory_space=pltpu.VMEM)
    dma = pltpu.SemaphoreType.DMA
    (both,) = pl.pallas_call(
        functools.partial(kernel, n_atom, n_mode),
        out_shape=(
            jax.ShapeDtypeStruct((2, MODE_DEV), F32),
        ),
        in_specs=[any_spec] * 6,
        out_specs=(vmem_spec,),
        scratch_shapes=[
            pltpu.VMEM((3, ATOM_DEV, MODE_DEV), BF16),
            pltpu.VMEM((3, 3, NBR, ATOM_DEV), F32),
            pltpu.VMEM((3, NBR, ATOM_DEV), F32),
            pltpu.VMEM((NBR, ATOM_DEV), jnp.int32),
            pltpu.VMEM((2, MODE_DEV), jnp.int32),
            pltpu.VMEM((n_mode, MODE_DEV), F32),
            pltpu.VMEM((2, 3, RIM, HALF), BF16),
            pltpu.VMEM((2, 3, RIM, HALF), BF16),
            pltpu.VMEM((3, ATOM_DEV, HALF), BF16),
            pltpu.VMEM((3, ATOM_DEV, HALF), BF16),
            pltpu.VMEM((ATOM_DEV, NBR), F32),
            pltpu.VMEM((GROUPS, 256, ATOM_DEV), BF16),
            pltpu.VMEM((GROUPS, 27 * GROUP, 256), BF16),
            pltpu.VMEM((9, ATOM_DEV, 3 * ATOM_DEV), BF16),
            pltpu.VMEM((9, ATOM_DEV, 3 * RIM), BF16),
            pltpu.VMEM((2, 3, ATOM_DEV, HALF), BF16),
            pltpu.VMEM((MODE_DEV + 2 * HALF, 3 * ATOM_DEV), BF16),
            pltpu.VMEM((2, n_atom, 3, 2, ROWS, HALF), BF16),
            pltpu.VMEM((2, n_atom - 1, 3, 2, ROWS, HALF), BF16),
            pltpu.VMEM((MODE_DEV + 2 * HALF, HALF), F32),
            pltpu.VMEM((2, HALF), F32),
            pltpu.VMEM((n_atom - 1, 2, HALF), F32),
            pltpu.VMEM((1, HALF), F32),
            pltpu.VMEM((n_mode - 1, n_atom, 1, HALF), F32),
            pltpu.VMEM((9, ATOM_DEV, MODE_DEV), F32),
            dma((6,)),
            dma((2, 2)),
            dma((2, 2)),
            dma((2,)),
            dma((2,)),
            dma(()),
            dma(()),
            dma((2,)),
            dma((2,)),
            dma(()),
            dma(()),
            dma((n_mode - 1,)),
            dma((n_mode - 1,)),
            pltpu.SemaphoreType.REGULAR((5,)),
        ],
        compiler_params=pltpu.CompilerParams(
            collective_id=0, has_side_effects=True, vmem_limit_bytes=40 * 1024 * 1024
        ),
    )(*(pltpu.with_memory_space_constraint(part, pltpu.HBM) for part in operands))
    return both[0], both[1]


def solution(mesh):
    in_specs = (
        P(None, "atom", "mode"),
        P(None, None, None, "atom"),
        P(None, None, "atom"),
        P(None, "atom"),
        P(None, "mode"),
        P("mode"),
    )
    out_specs = (P("mode"), P("mode"))
    return jax.shard_map(body, mesh=mesh, in_specs=in_specs, out_specs=out_specs, check_vma=False)
```

```python
import functools
import math

import jax
import jax.numpy as jnp
from jax import lax
from jax.experimental import pallas as pl
from jax.experimental.pallas import tpu as pltpu
from jax.sharding import PartitionSpec as P

ATOM_DEV = 256
MODE_DEV = 256
NBR = 16
RIM = 128
HALF = 128
BROAD = 128
GROUP = 16
GROUPS = ATOM_DEV // GROUP
ROWS = 8
SIDE = 4
FAR_FIRST = sorted(
    ((dx, dy) for dx in range(SIDE) for dy in range(SIDE) if dx or dy),
    key=lambda step: -sum(min(part, SIDE - part) for part in step),
)
BF16 = jnp.bfloat16
F32 = jnp.float32
MESH = pl.DeviceIdType.MESH


def iota(shape, dim):
    return lax.broadcasted_iota(jnp.int32, shape, dim)


def contract(lhs, rhs, lhs_dim, rhs_dim):
    return lax.dot_general(
        lhs, rhs, (((lhs_dim,), (rhs_dim,)), ((), ())), preferred_element_type=F32
    )


def drain(ref, sem):
    pltpu.make_async_copy(ref, ref, sem).wait()


def kernel(
    n_atom,
    n_mode,
    eig_hbm,
    force_hbm,
    bond_hbm,
    nbr_hbm,
    band_hbm,
    freq_hbm,
    out_ref,
    eig,
    force,
    bond,
    nbr,
    band,
    spectrum,
    low_rows,
    high_rows,
    low_cols,
    high_cols,
    nbr_cols,
    hot,
    spread,
    own_m,
    rim_m,
    flux,
    eig_t,
    send_pair,
    recv_pair,
    freq_col,
    send_sum,
    recv_sum,
    send_total,
    recv_total,
    inner_flux,
    local_sem,
    row_send,
    row_recv,
    col_send,
    col_recv,
    freq_send,
    freq_recv,
    pair_send,
    pair_recv,
    sum_send,
    sum_recv,
    total_send,
    total_recv,
    ready,
):
    me = lax.axis_index("atom")
    block = lax.axis_index("mode")
    atoms = n_atom * ATOM_DEV

    barrier = pltpu.get_barrier_semaphore()

    recv_total[...] = jnp.zeros_like(recv_total)
    x, y = me & (SIDE - 1), me // SIDE

    def across(dx, dy):
        return ((y + dy) & (SIDE - 1)) * SIDE + ((x + dx) & (SIDE - 1))

    adjacent = (across(1, 0), across(SIDE - 1, 0), across(0, 1), across(0, SIDE - 1))
    peers = [across(dx, dy) for dx, dy in FAR_FIRST]
    ring = (lax.rem(me + 1, n_atom), lax.rem(me + n_atom - 1, n_atom))

    def signal(sem, atom, mode):
        pl.semaphore_signal(sem, inc=1, device_id=(atom, mode), device_id_type=MESH)

    for peer in adjacent + ring:
        signal(barrier, peer, block)

    def beside(shift, action):
        @pl.when(block + shift < n_mode)
        def _():
            action(block + shift)

        @pl.when(block - shift >= 0)
        def _():
            action(block - shift)

    beside(1, lambda other: signal(barrier, me, other))

    loads = [
        pltpu.make_async_copy(nbr_hbm, nbr, local_sem.at[0]),
        pltpu.make_async_copy(bond_hbm, bond, local_sem.at[1]),
        pltpu.make_async_copy(force_hbm, force, local_sem.at[2]),
        pltpu.make_async_copy(eig_hbm, eig, local_sem.at[3]),
        pltpu.make_async_copy(band_hbm, band, local_sem.at[4]),
        pltpu.make_async_copy(freq_hbm, spectrum.at[pl.ds(0, 1), :], local_sem.at[5]),
    ]
    for load in loads:
        load.start()

    lane = iota((ATOM_DEV, 256), 1)
    diagonal = (iota((ATOM_DEV, 256), 0) & (GROUP - 1)) == (lane & (GROUP - 1))
    slot_rows = jnp.where(
        (iota((NBR, 256), 1) >> 4) == iota((NBR, 256), 0), 1.0, 0.0
    ).astype(BF16)

    loads[0].wait()
    atom_ids = iota((NBR, ATOM_DEV), 1)
    offset = ((nbr[...] - me * ATOM_DEV - atom_ids + RIM + atoms) & (atoms - 1)) - RIM
    column = jnp.where(offset == RIM, atom_ids, (atom_ids + offset) & (ATOM_DEV - 1))
    nbr_cols[...] = column.astype(F32).T

    pl.semaphore_wait(
        barrier,
        6 + (block > 0).astype(jnp.int32) + (block < n_mode - 1).astype(jnp.int32),
    )

    def to_atom(src, dst, q, send, recv):
        return pltpu.make_async_remote_copy(
            src_ref=src,
            dst_ref=dst,
            send_sem=send,
            recv_sem=recv,
            device_id=(lax.rem(me + q, n_atom), block),
            device_id_type=MESH,
        )

    def to_mode(src, dst, q, send, recv):
        return pltpu.make_async_remote_copy(
            src_ref=src,
            dst_ref=dst,
            send_sem=send,
            recv_sem=recv,
            device_id=(me, lax.rem(block + q, n_mode)),
            device_id_type=MESH,
        )

    def rim_copies(h):
        cols = pl.ds(h * HALF, HALF)
        up = to_atom(
            eig_hbm.at[:, pl.ds(ATOM_DEV - RIM, RIM), cols],
            low_rows.at[h],
            1,
            row_send.at[h, 0],
            row_recv.at[h, 0],
        )
        down = to_atom(
            eig_hbm.at[:, pl.ds(0, RIM), cols],
            high_rows.at[h],
            n_atom - 1,
            row_send.at[h, 1],
            row_recv.at[h, 1],
        )
        return up, down

    rims = rim_copies(0) + rim_copies(1)
    up_cols = to_mode(
        eig_hbm.at[:, :, pl.ds(MODE_DEV - HALF, HALF)], low_cols, 1, col_send.at[0], col_recv.at[0]
    )
    down_cols = to_mode(
        eig_hbm.at[:, :, pl.ds(0, HALF)], high_cols, n_mode - 1, col_send.at[1], col_recv.at[1]
    )
    for rim in rims:
        rim.start()

    @pl.when(block < n_mode - 1)
    def _():
        up_cols.start()

    @pl.when(block > 0)
    def _():
        down_cols.start()

    for peer in adjacent:
        signal(ready.at[2], peer, block)

    def send_freq(q, carry):
        to_mode(
            spectrum.at[pl.ds(0, 1), :],
            spectrum.at[pl.ds(q, 1), :],
            q,
            freq_send,
            freq_recv,
        ).start()
        return carry


    col_ids = iota((GROUP, ATOM_DEV), 1).astype(F32)

    def one_hot(g, carry):
        own_cols = nbr_cols[pl.ds(pl.multiple_of(g * GROUP, GROUP), GROUP), :]
        for n in range(NBR):
            hot[g, n * GROUP : (n + 1) * GROUP, :] = jnp.where(
                own_cols[:, n : n + 1] == col_ids, 1.0, 0.0
            ).astype(BF16)
        return carry

    lax.fori_loop(0, GROUPS, one_hot, 0, unroll=8)

    loads[5].wait()

    @pl.when(block > 0)
    def _():
        pl.semaphore_wait(ready.at[0], 1)

    @pl.when(block < n_mode - 1)
    def _():
        signal(ready.at[0], me, block + 1)

    def tell(sem):
        def one(other, carry):
            signal(sem, me, other)
            return carry

        lax.fori_loop(0, block, one, 0)

    def hear(sem):
        @pl.when(block < n_mode - 1)
        def _():
            pl.semaphore_wait(sem, n_mode - 1 - block)

    tell(ready.at[4])
    lax.fori_loop(n_mode - block, n_mode, send_freq, 0)
    loads[1].wait()
    loads[2].wait()

    def spread_out():
        for k in range(3):
            for c in range(3):
                for d in range(3):
                    coupling = (bond[k] * force[c, d]).astype(BF16)
                    wide = jnp.where(diagonal, contract(coupling, slot_rows, 0, 0), 0.0)
                    first = (9 * k + 3 * c + d) * GROUP
                    spread[:, first : first + GROUP, :] = wide.astype(BF16).reshape(
                        GROUPS, GROUP, 256
                    )

    near = iota((GROUP, RIM), 1) - iota((GROUP, RIM), 0)

    def unfold(h, g):
        dense = contract(spread[g], hot[g], 1, 0)
        gap = near - (g - h * (GROUPS // 2)) * GROUP
        below, same = gap < 0, gap == 0
        rows = pl.ds(pl.multiple_of(g * GROUP, GROUP), GROUP)
        for q in range(9):
            for d in range(3):
                first = (3 * q + d) * GROUP
                left = dense[first : first + GROUP, :RIM]
                right = dense[first : first + GROUP, RIM:]
                if h == 0:
                    own_left = jnp.where(same, 0.0, left)
                    own_right = jnp.where(below, right, jnp.where(same, left, 0.0))
                    rim = jnp.where(below, 0.0, right)
                else:
                    own_left = jnp.where(below, 0.0, left)
                    own_right = jnp.where(same, 0.0, right)
                    rim = jnp.where(below, left, jnp.where(same, right, 0.0))
                own_m[q, rows, d * ATOM_DEV : d * ATOM_DEV + RIM] = own_left.astype(BF16)
                own_m[q, rows, d * ATOM_DEV + RIM : (d + 1) * ATOM_DEV] = own_right.astype(BF16)
                rim_m[q, rows, d * RIM : (d + 1) * RIM] = rim.astype(BF16)

    def build():
        for h in range(2):

            def group(g, carry, h=h):
                unfold(h, g)
                return carry

            lax.fori_loop(
                h * (GROUPS // 2), (h + 1) * (GROUPS // 2), group, 0, unroll=True
            )

    row = iota((HALF, HALF), 0)
    col = iota((HALF, HALF), 1)

    def inner_part_of(k):
        inner_flux[3 * k : 3 * k + 3] = contract(
            own_m[3 * k : 3 * k + 3].reshape(3 * ATOM_DEV, 3 * ATOM_DEV),
            eig[...].reshape(3 * ATOM_DEV, MODE_DEV),
            1,
            0,
        ).reshape(3, ATOM_DEV, MODE_DEV)

    def project(h, k):
        ours = slice(h * HALF, (h + 1) * HALF)
        for side, halo in enumerate((low_rows, high_rows)):
            rows = slice(side * RIM, (side + 1) * RIM)
            outer = contract(
                rim_m[3 * k : 3 * k + 3, rows, :].reshape(3 * RIM, 3 * RIM),
                halo[h].reshape(3 * RIM, HALF),
                1,
                0,
            ).reshape(3, RIM, HALF)
            flux[h, :, rows, :] = (inner_flux[3 * k : 3 * k + 3, rows, ours] + outer).astype(BF16)
        pair = contract(
            eig_t[h * HALF : (h + 3) * HALF], flux[h].reshape(3 * ATOM_DEV, HALF), 1, 0
        )
        before, level, after = (pair[s * HALF : (s + 1) * HALF] for s in range(3))
        outer = jnp.where(row > col, before, after)
        inner_part = jnp.where(row == col, before, level)
        send_pair[h, :, k, 0] = outer.reshape(n_atom, ROWS, HALF).astype(BF16)
        send_pair[h, :, k, 1] = inner_part.reshape(n_atom, ROWS, HALF).astype(BF16)

    def scatter(h):
        for slot, peer in enumerate(peers):
            pltpu.make_async_remote_copy(
                src_ref=send_pair.at[h, peer],
                dst_ref=recv_pair.at[h, slot],
                send_sem=pair_send.at[h],
                recv_sem=pair_recv.at[h],
                device_id=(peer, block),
                device_id_type=MESH,
            ).start()

    spread_out()
    pl.semaphore_wait(ready.at[2], len(adjacent))
    signal(ready.at[3], across(2, 0), block)
    signal(ready.at[3], across(0, 2), block)
    build()
    loads[3].wait()
    for k in range(3):
        inner_part_of(k)
    for c in range(3):
        eig_t[HALF : HALF + MODE_DEV, c * ATOM_DEV : (c + 1) * ATOM_DEV] = eig[c].T

    @pl.when(block > 0)
    def _():
        up_cols.wait_recv()

    @pl.when(block == 0)
    def _():
        low_cols[...] = jnp.zeros_like(low_cols)

    @pl.when(block < n_mode - 1)
    def _():
        down_cols.wait_recv()

    @pl.when(block == n_mode - 1)
    def _():
        high_cols[...] = jnp.zeros_like(high_cols)

    for c in range(3):
        eig_t[:HALF, c * ATOM_DEV : (c + 1) * ATOM_DEV] = low_cols[c].T
        eig_t[HALF + MODE_DEV :, c * ATOM_DEV : (c + 1) * ATOM_DEV] = high_cols[c].T
    for rim in rims[:2]:
        rim.wait_recv()
    for k in range(3):
        project(0, k)
    pl.semaphore_wait(ready.at[3], 2)
    scatter(0)
    tell(ready.at[1])
    for rim in rims[2:]:
        rim.wait_recv()
    for k in range(3):
        project(1, k)
    scatter(1)
    hear(ready.at[4])
    lax.fori_loop(1, n_mode - block, send_freq, 0)

    loads[4].wait()
    drain(spectrum.at[pl.ds(1, n_mode - 1), :], freq_recv)
    own_freq = spectrum[pl.ds(0, 1), :]
    columns = spectrum[...].T
    freq_col[:HALF] = jnp.broadcast_to(columns[HALF:, 1:2], (HALF, HALF))
    freq_col[HALF : HALF + MODE_DEV] = jnp.broadcast_to(columns[:, 0:1], (MODE_DEV, HALF))
    freq_col[HALF + MODE_DEV :] = jnp.broadcast_to(
        columns[:HALF, n_mode - 1 : n_mode], (HALF, HALF)
    )
    every = spectrum[...]
    highest = jnp.max(jnp.max(every, axis=1, keepdims=True), axis=0, keepdims=True)
    lowest = jnp.min(jnp.min(every, axis=1, keepdims=True), axis=0, keepdims=True)
    broaden = BROAD * (highest - lowest) / (n_mode * MODE_DEV - 1)

    start = block * MODE_DEV
    first = me * ROWS
    rows = first + iota((ROWS, HALF), 0)
    lanes = iota((ROWS, HALF), 1)
    weights = []
    for h in range(2):
        ours = slice(h * HALF, (h + 1) * HALF)
        mine = own_freq[:, ours]
        lower = band[0:1, ours]
        upper = band[1:2, ours]

        def freq_at(offset):
            return freq_col[pl.ds(pl.multiple_of(offset + first, ROWS), ROWS), :]

        before = freq_at(h * HALF)
        level = freq_at((h + 1) * HALF)
        after = freq_at((h + 2) * HALF)
        base = start + h * HALF + rows
        for partner, ids in (
            (
                jnp.where(rows > lanes, before, after),
                base + jnp.where(rows > lanes, -HALF, HALF),
            ),
            (
                jnp.where(rows == lanes, before, level),
                base + jnp.where(rows == lanes, -HALF, 0),
            ),
        ):
            own_ids = start + h * HALF + lanes
            inside = (ids >= lower) & (ids < upper) & (ids != own_ids)
            detune = mine - partner
            lorentz = broaden / math.pi / (detune * detune + broaden * broaden)
            factor = (mine + partner) ** 2 / (4.0 * mine * partner)
            weights.append((inside, lorentz * factor))

    for h in range(2):
        drain(recv_pair.at[h], pair_recv.at[h])
        total = send_pair[h, me].astype(F32)
        for q in range(n_atom - 1):
            total = total + recv_pair[h, q].astype(F32)
        strength = jnp.sum(total * total, axis=0)
        term = 0.0
        for s in range(2):
            inside, weight = weights[2 * h + s]
            term = term + jnp.where(inside, weight * strength[s], 0.0)
        send_sum[h : h + 1] = jnp.sum(term, axis=0, keepdims=True)

    for slot, peer in enumerate(peers):
        pltpu.make_async_remote_copy(
            src_ref=send_sum,
            dst_ref=recv_sum.at[slot],
            send_sem=sum_send,
            recv_sem=sum_recv,
            device_id=(peer, block),
            device_id_type=MESH,
        ).start()
    freq_two = jnp.concatenate([own_freq[:, :HALF], own_freq[:, HALF:]], axis=0)
    grown = jnp.exp(freq_two)
    capacity = freq_two * freq_two * grown / ((grown - 1.0) * (grown - 1.0))
    prefactor = math.pi / (3.0 * freq_two * freq_two)
    part_total = capacity * prefactor * send_sum[...]
    send_total[...] = part_total[0:1] + part_total[1:2]

    def share_total(shift):
        for slot, peer in enumerate(peers + [me]):
            pltpu.make_async_remote_copy(
                src_ref=send_total,
                dst_ref=recv_total.at[shift - 1, pl.ds(slot, 1), :],
                send_sem=total_send.at[shift - 1],
                recv_sem=total_recv.at[shift - 1],
                device_id=(peer, block + shift),
                device_id_type=MESH,
            ).start()

    hear(ready.at[1])
    for shift in range(n_mode - 1, 0, -1):
        pl.when(block + shift < n_mode)(functools.partial(share_total, shift))
    drain(recv_sum, sum_recv)
    row_sums = send_sum[...]
    for q in range(n_atom - 1):
        row_sums = row_sums + recv_sum[q]
    diffusivity = prefactor * row_sums
    out_ref[0:1, :HALF] = diffusivity[0:1]
    out_ref[0:1, HALF:] = diffusivity[1:2]
    running = capacity * diffusivity
    lane_two = iota((2, HALF), 1)
    for step in (1, 2, 4, 8, 16, 32, 64):
        running = running + jnp.where(lane_two >= step, pltpu.roll(running, step, 1), 0.0)
    low_total = running[0:1, HALF - 1 : HALF]
    running = running + jnp.where(iota((2, HALF), 0) == 1, low_total, 0.0)

    def hear_total(t, carry):
        drain(recv_total.at[t], total_recv.at[t])
        return carry

    lax.fori_loop(0, block, hear_total, 0)
    earlier = jnp.sum(
        jnp.sum(jnp.sum(recv_total[...], axis=0), axis=0, keepdims=True), axis=1, keepdims=True
    )
    conductivity = (earlier + running) / MODE_DEV
    out_ref[1:2, :HALF] = conductivity[0:1]
    out_ref[1:2, HALF:] = conductivity[1:2]

    for rim in rims:
        rim.wait_send()

    @pl.when(block < n_mode - 1)
    def _():
        up_cols.wait_send()

    @pl.when(block > 0)
    def _():
        down_cols.wait_send()

    drain(spectrum.at[pl.ds(1, n_mode - 1), :], freq_send)
    for h in range(2):
        drain(recv_pair.at[h], pair_send.at[h])
    drain(recv_sum, sum_send)

    def sent_total(t, carry):
        drain(recv_total.at[t], total_send.at[t])
        return carry

    lax.fori_loop(0, n_mode - 1 - block, sent_total, 0)


def body(eigvec, force, bond, nbr, band, freq):
    n_atom, n_mode = lax.axis_size("atom"), lax.axis_size("mode")
    operands = (eigvec, force, bond, nbr, band, freq.reshape(1, MODE_DEV))
    any_spec = pl.BlockSpec(memory_space=pl.ANY)
    vmem_spec = pl.BlockSpec(memory_space=pltpu.VMEM)
    dma = pltpu.SemaphoreType.DMA
    (both,) = pl.pallas_call(
        functools.partial(kernel, n_atom, n_mode),
        out_shape=(
            jax.ShapeDtypeStruct((2, MODE_DEV), F32),
        ),
        in_specs=[any_spec] * 6,
        out_specs=(vmem_spec,),
        scratch_shapes=[
            pltpu.VMEM((3, ATOM_DEV, MODE_DEV), BF16),
            pltpu.VMEM((3, 3, NBR, ATOM_DEV), F32),
            pltpu.VMEM((3, NBR, ATOM_DEV), F32),
            pltpu.VMEM((NBR, ATOM_DEV), jnp.int32),
            pltpu.VMEM((2, MODE_DEV), jnp.int32),
            pltpu.VMEM((n_mode, MODE_DEV), F32),
            pltpu.VMEM((2, 3, RIM, HALF), BF16),
            pltpu.VMEM((2, 3, RIM, HALF), BF16),
            pltpu.VMEM((3, ATOM_DEV, HALF), BF16),
            pltpu.VMEM((3, ATOM_DEV, HALF), BF16),
            pltpu.VMEM((ATOM_DEV, NBR), F32),
            pltpu.VMEM((GROUPS, 256, ATOM_DEV), BF16),
            pltpu.VMEM((GROUPS, 27 * GROUP, 256), BF16),
            pltpu.VMEM((9, ATOM_DEV, 3 * ATOM_DEV), BF16),
            pltpu.VMEM((9, ATOM_DEV, 3 * RIM), BF16),
            pltpu.VMEM((2, 3, ATOM_DEV, HALF), BF16),
            pltpu.VMEM((MODE_DEV + 2 * HALF, 3 * ATOM_DEV), BF16),
            pltpu.VMEM((2, n_atom, 3, 2, ROWS, HALF), BF16),
            pltpu.VMEM((2, n_atom - 1, 3, 2, ROWS, HALF), BF16),
            pltpu.VMEM((MODE_DEV + 2 * HALF, HALF), F32),
            pltpu.VMEM((2, HALF), F32),
            pltpu.VMEM((n_atom - 1, 2, HALF), F32),
            pltpu.VMEM((1, HALF), F32),
            pltpu.VMEM((n_mode - 1, n_atom, HALF), F32),
            pltpu.VMEM((9, ATOM_DEV, MODE_DEV), F32),
            dma((6,)),
            dma((2, 2)),
            dma((2, 2)),
            dma((2,)),
            dma((2,)),
            dma(()),
            dma(()),
            dma((2,)),
            dma((2,)),
            dma(()),
            dma(()),
            dma((n_mode - 1,)),
            dma((n_mode - 1,)),
            pltpu.SemaphoreType.REGULAR((5,)),
        ],
        compiler_params=pltpu.CompilerParams(
            collective_id=0, has_side_effects=True, vmem_limit_bytes=40 * 1024 * 1024
        ),
    )(*(pltpu.with_memory_space_constraint(part, pltpu.HBM) for part in operands))
    return both[0], both[1]


def solution(mesh):
    in_specs = (
        P(None, "atom", "mode"),
        P(None, None, None, "atom"),
        P(None, None, "atom"),
        P(None, "atom"),
        P(None, "mode"),
        P("mode"),
    )
    out_specs = (P("mode"), P("mode"))
    return jax.shard_map(body, mesh=mesh, in_specs=in_specs, out_specs=out_specs, check_vma=False)
```
